256 devices in a mesh: dp: 16 (over z, core), mp: 16 (over y, x).
Axes of the slice: x: 4, y: 4, z: 8, core: 2. Of those that a mesh axis runs over, the one named last changes fastest.
Arguments:
- tokens: bfloat16 [49152, 8192], P('dp', 'mp'), may hold values from -6 to 6
- frozen_weight: bfloat16 [8192, 2048], P('mp', 'dp'), may hold values from -0.0625 to 0.0625
- adapter_down_weight: bfloat16 [8192, 4096], P(None, 'mp'), may hold values from -0.0625 to 0.0625
- adapter_up_weight: bfloat16 [2, 128, 16, 1024], P(None, 'mp'), may hold values from -1.5 to 1.5
- token_adapter_index: int32 [49152], P('dp'), may hold values from 0 to 127, as said below
Outputs:
- projected: bfloat16 [49152, 2048], P(('dp', 'mp'))
The draws below stay inside these ranges and needn't reach their ends.
Inputs may be any that keep to these rules, and one draw needn't show every extreme that they name: `token_adapter_index`: A token's owner is its adapter id divided by 8, rounded down. Of the 192 tokens of each aligned block of rows (the rows of one device's output), at most 24 have the same owner; in each run of 16 such blocks that one dp index holds, one owner has exactly 24 tokens in every block.
All inputs are finite; a program needn't handle non-finite values.
Results may differ from the reference program's by a relative error of at most 0.0055.
Values may be sent and summed in bfloat16 or wider, within the bound.
A program may use at most 128 MiB of HBM per device.

```python
import jax
import jax.numpy as jnp
from jax import lax

MODEL_DIM = 8192
KEY_VALUE_WIDTH = 1024
ADAPTER_RANK = 16
A_DEV = 8
TOK_DEV = 192
CAP = 24
ADAPTER_COUNT = 128
TOKENS = 49152


def draw_token_adapter_index(key, part):
    owner_count = ADAPTER_COUNT // A_DEV
    block_total = TOKENS // TOK_DEV

    def one_block(block_number):
        group_key = jax.random.fold_in(key, 1000003 + block_number // owner_count)
        hot_owner = jax.random.randint(group_key, (), 0, owner_count).astype(jnp.int32)
        block_key = jax.random.fold_in(key, block_number)
        key_place, key_order, key_pick = jax.random.split(block_key, 3)
        spread = jnp.arange((owner_count - 1) * CAP, dtype=jnp.int32) // CAP
        other_owners = (hot_owner + 1 + spread) % owner_count
        other_owners = jax.random.permutation(key_order, other_owners)
        ordered_owners = jnp.concatenate([jnp.full((CAP,), hot_owner, jnp.int32), other_owners[:TOK_DEV - CAP]])
        placement = jax.random.permutation(key_place, TOK_DEV)
        chosen_owner = jnp.zeros((TOK_DEV,), jnp.int32).at[placement].set(ordered_owners)
        picked = jax.random.randint(key_pick, (TOK_DEV,), 0, A_DEV).astype(jnp.int32)
        return chosen_owner * A_DEV + picked
    return jax.vmap(one_block)(jnp.arange(block_total, dtype=jnp.int32)).reshape(-1).astype(jnp.int32)


def raised(drawn, key, source, target, shards_of, factor):
    owner, partner = [(jnp.arange(drawn.shape[position]) // (drawn.shape[position] // shards_of)).reshape([-1 if axis == position else 1 for axis in range(drawn.ndim)]) for position in (source, target)]
    chosen = jax.random.permutation(key, shards_of)[partner]
    strong = (owner == chosen) | (owner == (partner + shards_of // 2) % shards_of)
    return jnp.where(strong, factor * drawn, drawn)


def steps_of(key, dims, cuts, smallest, high):
    factor_of, own = 1.0, jax.random.fold_in(key, 6)
    for position, blocks in cuts:
        draws = jnp.exp(jax.random.uniform(jax.random.fold_in(own, position), (blocks,), jnp.float32, smallest / len(cuts), high / len(cuts)))
        factor_of = factor_of * jnp.repeat(draws, dims[position] // blocks).reshape([-1 if axis == position else 1 for axis in range(len(dims))])
    return factor_of


def scatter_about(own_key, shape, scale, limit, shards=(), kind=jnp.bfloat16):
    loudness = steps_of(own_key, shape, shards, -0.22, 0.18) if shards else 1.0
    array = jax.random.normal(own_key, shape, jnp.float32) * scale * loudness
    return jnp.minimum(jnp.maximum(array, -limit), limit).astype(kind)


def gaussian_with(own_key, shape, scale, most, cuts, heavy, held_as=jnp.bfloat16):
    values = scale * jax.random.normal(own_key, shape, jnp.float32)
    if cuts:
        values = values * steps_of(own_key, shape, cuts, -0.22, 0.18)
    return jnp.clip(raised(values, jax.random.fold_in(own_key, 3), *heavy), -most, most).astype(held_as)


def setup_inputs(seed: int = 0) -> dict:
    splits = jax.random.split(jax.random.key(seed), 6)
    tokens = gaussian_with(splits[0], (TOKENS, MODEL_DIM), 1.0, 6.0, ((0, 16), (1, 16)), (1, 0, 16, 2.0))
    frozen_weight = scatter_about(splits[1], (MODEL_DIM, 2 * KEY_VALUE_WIDTH), MODEL_DIM ** -0.5, 0.0625, ((0, 16), (1, 16)))
    adapter_down_weight = scatter_about(splits[2], (MODEL_DIM, ADAPTER_COUNT * 2 * ADAPTER_RANK), MODEL_DIM ** -0.5, 0.0625, ((1, 16),))
    adapter_up_weight = scatter_about(splits[3], (2, ADAPTER_COUNT, ADAPTER_RANK, KEY_VALUE_WIDTH), ADAPTER_RANK ** -0.5, 1.5, ((1, 16),))
    token_adapter_index = draw_token_adapter_index(jax.random.fold_in(splits[5], 71), 0)
    return dict(tokens=tokens, frozen_weight=frozen_weight, adapter_down_weight=adapter_down_weight, adapter_up_weight=adapter_up_weight, token_adapter_index=token_adapter_index)


ADAPTER_SCALE = 2.0


def reference(tokens, frozen_weight, adapter_down_weight, adapter_up_weight, token_adapter_index):
    base_out = jnp.dot(tokens, frozen_weight, preferred_element_type=jnp.float32)
    block_count = TOKENS // TOK_DEV
    token_blocks = tokens.reshape(block_count, TOK_DEV, MODEL_DIM)
    id_blocks = token_adapter_index.reshape(block_count, TOK_DEV)
    down_tensor = adapter_down_weight.reshape(MODEL_DIM, ADAPTER_COUNT, 2 * ADAPTER_RANK)

    def adapt_block(block_pair):
        block_rows, block_labels_list = block_pair
        down_rows = jnp.take(down_tensor, block_labels_list, axis=1).astype(jnp.float32)
        low_rank = jnp.einsum("td,dtr->tr", block_rows.astype(jnp.float32), down_rows).astype(jnp.bfloat16)
        up_weight_rows = jnp.take(adapter_up_weight, block_labels_list, axis=1).astype(jnp.float32)
        low_parts = low_rank.astype(jnp.float32).reshape(TOK_DEV, 2, ADAPTER_RANK)
        adapter_updates = jnp.einsum("tpr,ptrk->tpk", low_parts, up_weight_rows).reshape(TOK_DEV, 2 * KEY_VALUE_WIDTH)
        return (ADAPTER_SCALE * adapter_updates).astype(jnp.bfloat16)

    adapter_updates = lax.map(adapt_block, (token_blocks, id_blocks)).reshape(TOKENS, 2 * KEY_VALUE_WIDTH)
    return (base_out + adapter_updates.astype(jnp.float32)).astype(jnp.bfloat16)
```

```python
import jax
import jax.numpy as jnp
from jax import lax
from jax.experimental import pallas as pl
from jax.experimental.pallas import tpu as pltpu
from jax.sharding import PartitionSpec as P

SIDE = 4
GROUP = SIDE * SIDE
ADAPTER_SCALE = 2.0
LANES = 128


def body(
    idx_ref, x_hbm, w_hbm, d_hbm, u_hbm, out_ref,
    x_v, xq, w_v, d_v, u_v, low_acc, key_low, key_up, p_send, p_recv, q_send, q_recv,
    e_v, acc_v, o_send, o_recv,
    l_sem, s_d, r_d, s_f, r_f, s_w, r_w, s_x, r_x, s_u, r_u, s_uf, r_uf,
    s_r, r_r, s_s, r_s, s_p, r_p, s_q, r_q, s_o, r_o,
):
    f32, bf16 = jnp.float32, jnp.bfloat16
    depth = w_hbm.shape[0]
    quarter = xq.shape[0]
    own = out_ref.shape[0]
    wide = w_v.shape[2]
    chips = w_v.shape[0]
    half_d = depth // 2
    half_w = w_v.shape[1] // 2
    up_rows = u_hbm.shape[1]

    dp, me = lax.axis_index("dp"), lax.axis_index("mp")
    z, c = dp // 2, dp % 2
    y, x = me // SIDE, me % SIDE
    sib = 2 * z + 1 - c

    def z_at(step):
        return (z + step + chips) % chips

    def y_peer(step):
        return ((y + step) % SIDE) * SIDE + x

    def x_peer(step):
        return y * SIDE + (x + step) % SIDE

    def remote(src, dst, send_sem, recv_sem, d, m):
        return pltpu.make_async_remote_copy(
            src_ref=src, dst_ref=dst, send_sem=send_sem, recv_sem=recv_sem,
            device_id=(d, m), device_id_type=pl.DeviceIdType.MESH,
        )

    barrier = pltpu.get_barrier_semaphore()

    def greet(d, m):
        pl.semaphore_signal(barrier, inc=1, device_id=(d, m), device_id_type=pl.DeviceIdType.MESH)

    @pl.loop(1, GROUP)
    def _(i):
        greet(dp, (me + i) % GROUP)

    for i in range(1, SIDE):
        greet(sib, y_peer(i))
    greet(sib, me)
    greet(2 * z_at(1) + c, me)
    greet(2 * z_at(-1) + c, me)

    x_local = pltpu.make_async_copy(x_hbm, x_v, l_sem.at[0])
    x_local.start()
    d_local = pltpu.make_async_copy(d_hbm.at[pl.ds(depth * me, depth), :], d_v.at[me], l_sem.at[1])
    d_local.start()
    pl.semaphore_wait(barrier, GROUP - 1 + SIDE - 1 + 3)

    to_core = y // 2
    w_slot = (y % 2) * 2 + c
    w_own = w_v.at[z, pl.ds(depth * y, depth), pl.ds(LANES * c, LANES)]

    def w_start(i):
        return remote(w_hbm, w_own, s_w.at[i], r_w.at[w_slot], 2 * z + to_core, y_peer(i))

    for i in range(1, SIDE):
        w_start(i).start()

    @pl.when(c == to_core)
    def _():
        pltpu.make_async_copy(w_hbm, w_own, r_w.at[w_slot]).start()

    @pl.when(c != to_core)
    def _():
        w_start(0).start()

    def d_copy(i):
        peer = (me + i) % GROUP
        return remote(
            d_hbm.at[pl.ds(depth * peer + half_d * c, half_d), :],
            d_v.at[me, pl.ds(half_d * c, half_d), :],
            s_d.at[i], r_d.at[i], dp, peer,
        )

    def d_arrival(i):
        source = (me - i + GROUP) % GROUP
        block = d_v.at[source, pl.ds(half_d * c, half_d), :]
        return remote(block, block, s_d.at[i], r_d.at[i], dp, me), block

    def d_forward(i, core):
        source = (me - i + GROUP) % GROUP
        block = d_v.at[source, pl.ds(half_d * core, half_d), :]
        return remote(block, block, s_f.at[i], r_f.at[i], sib, me)

    @pl.loop(1, GROUP)
    def _(i):
        d_copy(i).start()

    def x_copy(i):
        to = (y + i) % SIDE
        return remote(
            x_hbm.at[pl.ds(quarter * to, quarter), :], xq.at[:, pl.ds(depth * y, depth)],
            s_x.at[i], r_x.at[i], dp, y_peer(i),
        )

    def x_arrival(i):
        source = (y - i + SIDE) % SIDE
        block = xq.at[:, pl.ds(depth * source, depth)]
        return remote(block, block, s_x.at[i], r_x.at[i], dp, me)

    for i in range(1, SIDE):
        x_copy(i).start()
    xq_local = pltpu.make_async_copy(
        x_hbm.at[pl.ds(quarter * y, quarter), :], xq.at[:, pl.ds(depth * y, depth)], l_sem.at[2]
    )
    xq_local.start()

    u_own = u_v.at[c, pl.ds(up_rows * y, up_rows), :]

    def u_copy(i):
        return remote(u_hbm.at[c], u_own, s_u.at[i], r_u.at[i], dp, y_peer(i))

    def u_arrival(i):
        source = (y - i + SIDE) % SIDE
        block = u_v.at[c, pl.ds(up_rows * source, up_rows), :]
        return remote(block, block, s_u.at[i], r_u.at[i], dp, me)

    for i in range(1, SIDE):
        u_copy(i).start()
    u_local = pltpu.make_async_copy(u_hbm.at[c], u_own, l_sem.at[3])
    u_local.start()

    lane = lax.broadcasted_iota(jnp.int32, (LANES, LANES), 1)
    low_acc[...] = jnp.zeros_like(low_acc)

    def adapters(block):
        row = idx_ref[pl.ds(block, 1), :].astype(f32)
        return jnp.transpose(jnp.broadcast_to(row, (LANES, LANES))).astype(jnp.int32)

    @pl.loop(0, key_low.shape[0] // LANES)
    def _(b):
        a = adapters(b)
        key_low[pl.ds(pl.multiple_of(b * LANES, LANES), LANES), :] = jnp.where(
            (lane >> 5) == (a & 3), a >> 2, -1
        )

    @pl.loop(0, quarter // LANES)
    def _(b):
        a = adapters(y * (quarter // LANES) + b)
        owner = a >> 3
        mine = jnp.logical_and((owner & 3) == x, (lane >> 4) == (a & 7))
        key_up[pl.ds(pl.multiple_of(b * LANES, LANES), LANES), :] = jnp.where(mine, owner >> 2, -1)

    def half(block, core):
        return w_v.at[block, pl.ds(half_w * core, half_w), :]

    def ring(t, block, to):
        return remote(half(block, c), half(block, c), s_r.at[t], r_r.at[t], 2 * to + c, me)

    def share(t, block, core):
        return remote(half(block, core), half(block, core), s_s.at[t], r_s.at[t], sib, me)

    for slot in range(4):
        block = w_v.at[z, pl.ds(depth * (2 * c + slot // 2), depth), pl.ds(LANES * (slot % 2), LANES)]
        remote(block, block, s_w.at[0], r_w.at[slot], dp, me).wait_recv()
    ring(1, z, z_at(1)).start()
    ring(2, z, z_at(-1)).start()
    share(0, z, c).start()

    last_block = z_at(-3 + 6 * c)
    last_to = z_at(1 - 2 * c)

    def ring_step(s):
        ring(2 * s - 1, z_at(-s), z).wait_recv()
        if s < 3:
            ring(2 * s + 1, z_at(-s), z_at(1)).start()
        ring(2 * s, z_at(s), z).wait_recv()
        if s < 3:
            ring(2 * s + 2, z_at(s), z_at(-1)).start()
        else:
            ring(7, last_block, last_to).start()
        share(2 * s - 1, z_at(-s), c).start()
        share(2 * s, z_at(s), c).start()

    x_local.wait()
    d_local.wait()

    @pl.loop(1, GROUP + 1)
    def _(i):
        @pl.when(i < GROUP)
        def _():
            arrival, _ = d_arrival(i)
            arrival.wait_recv()
            d_forward(i, c).start()

        @pl.when(i >= 2)
        def _():
            d_forward(i - 1, 1 - c).wait_recv()

        for s in (1, 2, 3):
            @pl.when(i == 5 * s + 1)
            def _():
                ring_step(s)

        owner = (me - (i - 1) + GROUP) % GROUP

        @pl.loop(0, SIDE)
        def _(q):
            rows = pl.ds(pl.multiple_of(q * quarter, quarter), quarter)
            product = jnp.dot(x_v[rows, :], d_v[owner], preferred_element_type=f32)
            key = key_low[rows, :]
            low_acc[rows, :] += jnp.where(key == 2 * owner, product[:, :LANES], 0.0) + jnp.where(
                key == 2 * owner + 1, product[:, LANES:], 0.0
            )

    lane_own = lax.broadcasted_iota(jnp.int32, (own, LANES), 1)

    @pl.loop(0, SIDE)
    def _(q):
        packed = jnp.zeros((own, LANES), f32)
        for j in range(SIDE):
            v = low_acc[pl.ds(pl.multiple_of(q * quarter + j * own, own), own), :]
            v = v + pltpu.roll(v, 64, 1)
            v = v + pltpu.roll(v, 32, 1)
            packed = jnp.where((lane_own >> 5) == j, v, packed)
        p_send[q] = packed

    def p_copy(i):
        return remote(p_send.at[(y + i) % SIDE], p_recv.at[i - 1], s_p.at[i], r_p.at[i], dp, y_peer(i))

    def q_copy(i):
        return remote(q_send, q_recv.at[i - 1], s_q.at[i], r_q.at[i], dp, x_peer(i))

    for i in range(1, SIDE):
        p_copy(i).start()
    for i in range(1, SIDE):
        p_copy(i).wait_recv()
    q_send[...] = (p_send[y] + p_recv[0]) + (p_recv[1] + p_recv[2])
    for i in range(1, SIDE):
        q_copy(i).start()
    u_local.wait()
    for i in range(1, SIDE):
        u_arrival(i).wait_recv()

    def u_forward(core):
        return remote(u_v.at[core], u_v.at[core], s_uf, r_uf, sib, me)

    u_forward(c).start()
    for i in range(1, SIDE):
        q_copy(i).wait_recv()
    low = ((q_send[...] + q_recv[0]) + (q_recv[1] + q_recv[2])).astype(bf16)
    low = (low.astype(f32) * ADAPTER_SCALE).astype(bf16)
    k_iota = lax.broadcasted_iota(jnp.int32, (LANES, LANES), 0)
    for j in range(SIDE):
        key = key_up[j * own:(j + 1) * own, :]
        for p in range(2):
            spread = (k_iota == 32 * j + 16 * p + (lane & 15)).astype(f32).astype(bf16)
            rows = jnp.dot(low, spread, preferred_element_type=f32)
            for g in range(SIDE):
                e_v[p, j * own:(j + 1) * own, g * LANES:(g + 1) * LANES] = jnp.where(
                    key == g, rows, 0.0
                ).astype(bf16)

    xq_local.wait()
    for i in range(1, SIDE):
        x_arrival(i).wait_recv()
    u_forward(1 - c).wait_recv()

    per_part = u_v.shape[2] // wide

    def block_at(t):
        return z_at(jnp.where(t % 2 == 1, -((t + 1) // 2), t // 2))

    def o_copy(i, n):
        to = (x + i) % SIDE
        return remote(
            o_send.at[n, pl.ds(own * to, own), :], o_recv.at[i - 1, n],
            s_o.at[i, n], r_o.at[i, n], dp, x_peer(i),
        )

    @pl.loop(0, chips)
    def _(t):
        n = block_at(t)

        @pl.when(t == 3)
        def _():
            ring(7, z_at(4), z).wait_recv()
            share(7, z_at(4), c).start()

        share(t, n, 1 - c).wait_recv()
        p = n // per_part
        columns = pl.ds(pl.multiple_of((n % per_part) * wide, wide), wide)
        total = jnp.dot(xq[...], w_v[n], preferred_element_type=f32) + jnp.dot(
            e_v[p], u_v[p, :, columns], preferred_element_type=f32
        )
        acc_v[n] = total
        o_send[n] = total.astype(bf16)
        for i in range(1, SIDE):
            o_copy(i, n).start()

    @pl.loop(0, chips)
    def _(t):
        n = block_at(t)
        for i in range(1, SIDE):
            o_copy(i, n).wait_recv()
        total = acc_v[n, pl.ds(pl.multiple_of(own * x, own), own), :]
        for i in range(SIDE - 1):
            total = total + o_recv[i, n].astype(f32)
        out_ref[:, pl.ds(pl.multiple_of(wide * n, wide), wide)] = total.astype(bf16)

    for i in range(1, SIDE):
        w_start(i).wait_send()
        x_copy(i).wait_send()
        u_copy(i).wait_send()
        p_copy(i).wait_send()
        q_copy(i).wait_send()

    @pl.when(c != to_core)
    def _():
        w_start(0).wait_send()

    u_forward(c).wait_send()

    @pl.loop(1, GROUP)
    def _(i):
        d_copy(i).wait_send()
        d_forward(i, c).wait_send()

    @pl.loop(1, chips)
    def _(t):
        ring(t, z, z).wait_send()

    @pl.loop(0, chips)
    def _(t):
        share(t, z, c).wait_send()
        for i in range(1, SIDE):
            o_copy(i, t).wait_send()


def local(tokens, frozen_weight, adapter_down_weight, adapter_up_weight, token_adapter_index):
    rows, depth = tokens.shape
    core_columns = frozen_weight.shape[1]
    devices = lax.axis_size("dp")
    chips = devices // 2
    columns = devices * core_columns
    present, rank, span = adapter_up_weight.shape[1:]
    quarter, own = rows // SIDE, rows // GROUP
    owner_columns = adapter_down_weight.shape[1]
    f32, bf16 = jnp.float32, jnp.bfloat16
    idx = token_adapter_index.reshape(rows // LANES, LANES)
    up = adapter_up_weight.reshape(2, present * rank, span)
    anywhere = pl.BlockSpec(memory_space=pl.ANY)
    vmem = pl.BlockSpec(memory_space=pltpu.VMEM)
    dma = pltpu.SemaphoreType.DMA
    return pl.pallas_call(
        body,
        out_shape=jax.ShapeDtypeStruct((own, columns), bf16),
        in_specs=[vmem, anywhere, anywhere, anywhere, anywhere],
        out_specs=vmem,
        scratch_shapes=[
            pltpu.VMEM((rows, depth), bf16),
            pltpu.VMEM((quarter, SIDE * depth), bf16),
            pltpu.VMEM((chips, SIDE * depth, 2 * core_columns), bf16),
            pltpu.VMEM((GROUP, depth, owner_columns), bf16),
            pltpu.VMEM((2, SIDE * present * rank, span), bf16),
            pltpu.VMEM((rows, LANES), f32),
            pltpu.VMEM((rows, LANES), jnp.int32),
            pltpu.VMEM((quarter, LANES), jnp.int32),
            pltpu.VMEM((SIDE, own, LANES), f32),
            pltpu.VMEM((SIDE - 1, own, LANES), f32),
            pltpu.VMEM((own, LANES), f32),
            pltpu.VMEM((SIDE - 1, own, LANES), f32),
            pltpu.VMEM((2, quarter, SIDE * present * rank), bf16),
            pltpu.VMEM((chips, quarter, 2 * core_columns), f32),
            pltpu.VMEM((chips, quarter, 2 * core_columns), bf16),
            pltpu.VMEM((SIDE - 1, chips, own, 2 * core_columns), bf16),
            dma((4,)),
            dma((GROUP,)), dma((GROUP,)), dma((GROUP,)), dma((GROUP,)),
            dma((4,)), dma((4,)), dma((SIDE,)), dma((SIDE,)), dma((SIDE,)), dma((SIDE,)),
            dma, dma,
            dma((chips,)), dma((chips,)), dma((chips,)), dma((chips,)),
            dma((SIDE,)), dma((SIDE,)), dma((SIDE,)), dma((SIDE,)),
            dma((SIDE, chips)), dma((SIDE, chips)),
        ],
        compiler_params=pltpu.CompilerParams(
            collective_id=0, has_side_effects=True, vmem_limit_bytes=60 << 20
        ),
        name="projections",
    )(idx, tokens, frozen_weight, adapter_down_weight, up)


def solution(mesh):
    placed = (P("dp", "mp"), P("mp", "dp"), P(None, "mp"), P(None, "mp", None, None), P("dp"))
    return jax.shard_map(
        local, mesh=mesh, in_specs=placed, out_specs=P(("dp", "mp"), None), check_vma=False
    )
```

```python
import jax
import jax.numpy as jnp
from jax import lax
from jax.experimental import pallas as pl
from jax.experimental.pallas import tpu as pltpu
from jax.sharding import PartitionSpec as P

SIDE = 4
GROUP = SIDE * SIDE
ADAPTER_SCALE = 2.0
LANES = 128
EARLY = 12
TO = (2, 1, 3, 0)
PEERS = (
    (0, 1), (0, 3), (0, 2), (1, 0), (3, 0), (1, 1), (3, 3), (1, 3), (3, 1),
    (2, 0), (1, 2), (3, 2), (2, 2), (2, 1), (2, 3),
)
ORDER_Y = sum(p[0] << (2 * k) for k, p in enumerate(PEERS))
ORDER_X = sum(p[1] << (2 * k) for k, p in enumerate(PEERS))
FIRST = 3
WINDOW = 8
TOKENS_AT = 8
UP_AT = 12
RING_AT = (6, 2)


def body(
    idx_ref, x_hbm, w_hbm, d_hbm, u_hbm, out_ref,
    x_v, xq, w_v, d_v, u_v, low_acc, key_low, key_up, p_send, p_recv, q_send, q_recv,
    e_v, acc_v, o_send, o_recv, relay_send, relay_recv,
    l_sem, s_d, r_d, s_f, r_f, s_w, r_w, s_x, r_x, s_u, r_u, s_uf, r_uf,
    s_r, r_r, s_s, r_s, s_p, r_p, s_q, r_q, s_o, r_o, s_y, r_y,
):
    f32, bf16 = jnp.float32, jnp.bfloat16
    depth = w_hbm.shape[0]
    quarter = xq.shape[0]
    own = out_ref.shape[0]
    wide = w_v.shape[2]
    chips = w_v.shape[0]
    half_d = depth // 2
    half_w = w_v.shape[1] // 2
    up_rows = u_hbm.shape[1]

    dp, me = lax.axis_index("dp"), lax.axis_index("mp")
    z, c = dp // 2, dp % 2
    y, x = me // SIDE, me % SIDE
    sib = 2 * z + 1 - c

    def z_at(step):
        return (z + step + chips) % chips

    def y_peer(step):
        return ((y + step) % SIDE) * SIDE + x

    def x_peer(step):
        return y * SIDE + (x + step) % SIDE

    def remote(src, dst, send_sem, recv_sem, d, m):
        return pltpu.make_async_remote_copy(
            src_ref=src, dst_ref=dst, send_sem=send_sem, recv_sem=recv_sem,
            device_id=(d, m), device_id_type=pl.DeviceIdType.MESH,
        )

    barrier = pltpu.get_barrier_semaphore()

    def greet(d, m):
        pl.semaphore_signal(barrier, inc=1, device_id=(d, m), device_id_type=pl.DeviceIdType.MESH)

    @pl.loop(1, GROUP)
    def _(i):
        greet(dp, (me + i) % GROUP)

    for i in range(1, SIDE):
        greet(sib, y_peer(i))
    greet(sib, me)
    greet(2 * z_at(1) + c, me)
    greet(2 * z_at(-1) + c, me)

    x_local = pltpu.make_async_copy(x_hbm, x_v, l_sem.at[0])
    x_local.start()
    d_local = pltpu.make_async_copy(d_hbm.at[pl.ds(depth * me, depth), :], d_v.at[me], l_sem.at[1])
    d_local.start()
    pl.semaphore_wait(barrier, GROUP - 1 + SIDE - 1 + 3)

    to_core = y // 2
    w_slot = (y % 2) * 2 + c
    w_own = w_v.at[z, pl.ds(depth * y, depth), pl.ds(LANES * c, LANES)]

    def w_start(i):
        return remote(w_hbm, w_own, s_w.at[i], r_w.at[w_slot], 2 * z + to_core, y_peer(i))

    for i in range(1, SIDE):
        w_start(i).start()

    @pl.when(c == to_core)
    def _():
        pltpu.make_async_copy(w_hbm, w_own, r_w.at[w_slot]).start()

    @pl.when(c != to_core)
    def _():
        w_start(0).start()

    def d_peer(k, sign):
        dy, dx = (ORDER_Y >> (2 * k)) & 3, (ORDER_X >> (2 * k)) & 3
        return ((y + sign * dy + SIDE) % SIDE) * SIDE + (x + sign * dx + SIDE) % SIDE

    def d_copy(k):
        peer = d_peer(k, 1)
        return remote(
            d_hbm.at[pl.ds(depth * peer + half_d * c, half_d), :],
            d_v.at[me, pl.ds(half_d * c, half_d), :],
            s_d.at[k], r_d.at[k], dp, peer,
        )

    def d_arrival(k):
        block = d_v.at[d_peer(k, -1), pl.ds(half_d * c, half_d), :]
        return remote(block, block, s_d.at[k], r_d.at[k], dp, me)

    def d_forward(k, core):
        block = d_v.at[d_peer(k, -1), pl.ds(half_d * core, half_d), :]
        return remote(block, block, s_f.at[k], r_f.at[k], sib, me)

    for k in range(FIRST):
        d_copy(k).start()

    def x_block(row_y, column_y, g):
        to = (x + TO[g]) % SIDE
        return (
            x_hbm.at[pl.ds(quarter * row_y + own * to, own), :],
            xq.at[pl.ds(own * to, own), pl.ds(depth * column_y, depth)],
        )

    def x_copy(i, g):
        src, dst = x_block((y + i) % SIDE, y, g)
        return remote(src, dst, s_x.at[i, g], r_x.at[i, g], dp, y_peer(i))

    def x_arrival(i, g):
        _, dst = x_block(y, (y - i + SIDE) % SIDE, g)
        return remote(dst, dst, s_x.at[i, g], r_x.at[i, g], dp, me)

    xq_local = pltpu.make_async_copy(
        x_hbm.at[pl.ds(quarter * y, quarter), :], xq.at[:, pl.ds(depth * y, depth)], l_sem.at[2]
    )
    xq_local.start()

    u_own = u_v.at[c, pl.ds(up_rows * y, up_rows), :]

    def u_copy(i):
        return remote(u_hbm.at[c], u_own, s_u.at[i], r_u.at[i], dp, y_peer(i))

    def u_arrival(i):
        source = (y - i + SIDE) % SIDE
        block = u_v.at[c, pl.ds(up_rows * source, up_rows), :]
        return remote(block, block, s_u.at[i], r_u.at[i], dp, me)

    u_local = pltpu.make_async_copy(u_hbm.at[c], u_own, l_sem.at[3])
    u_local.start()

    def piece(block, core, sub):
        return w_v.at[block, pl.ds(half_w * core + depth * sub, depth), :]

    def ring(t, block, sub, to):
        part = piece(block, c, sub)
        return remote(part, part, s_r.at[t, sub], r_r.at[t, sub], 2 * to + c, me)

    def share(t, block, sub, core):
        part = piece(block, core, sub)
        return remote(part, part, s_s.at[t, sub], r_s.at[t, sub], sib, me)

    for sub in range(2):
        for side in range(2):
            block = w_v.at[z, pl.ds(depth * (2 * c + sub), depth), pl.ds(LANES * side, LANES)]
            remote(block, block, s_w.at[0], r_w.at[2 * sub + side], dp, me).wait_recv()
        if sub == 0:
            ring(1, z, sub, z_at(1)).start()
            ring(2, z, sub, z_at(-1)).start()
    for k in range(FIRST, WINDOW):
        d_copy(k).start()

    lane = lax.broadcasted_iota(jnp.int32, (LANES, LANES), 1)
    low_acc[...] = jnp.zeros_like(low_acc)

    def adapters(block):
        row = idx_ref[pl.ds(block, 1), :].astype(f32)
        return jnp.transpose(jnp.broadcast_to(row, (LANES, LANES))).astype(jnp.int32)

    @pl.loop(0, key_low.shape[0] // LANES)
    def _(b):
        a = adapters(b)
        key_low[pl.ds(pl.multiple_of(b * LANES, LANES), LANES), :] = jnp.where(
            (lane >> 5) == (a & 3), a >> 2, -1
        )

    @pl.loop(0, quarter // LANES)
    def _(b):
        a = adapters(y * (quarter // LANES) + b)
        owner = a >> 3
        mine = jnp.logical_and((owner & 3) == x, (lane >> 4) == (a & 7))
        key_up[pl.ds(pl.multiple_of(b * LANES, LANES), LANES), :] = jnp.where(mine, owner >> 2, -1)

    ring(1, z, 1, z_at(1)).start()
    ring(2, z, 1, z_at(-1)).start()
    for sub in range(2):
        share(0, z, sub, c).start()

    def ring_event(e):
        step, way = e // 4 + 1, e % 2
        sub = jnp.where(e < 12, (e // 2) % 2, way)
        t = jnp.where(e < 12, 2 * step - 1 + way, 7)
        block = z_at(jnp.where(way == 0, -step, step))
        ring(t, block, sub, z).wait_recv()

        @pl.when(jnp.logical_or(e < 8, jnp.logical_and(e < 12, way == c)))
        def _():
            ring(jnp.where(e < 8, t + 2, 7), block, sub, z_at(1 - 2 * way)).start()

        share(t, block, sub, c).start()

    def down_step(k, q):
        owner = jnp.where(k == 0, me, d_peer(jnp.maximum(k - 1, 0), -1))
        rows = pl.ds(pl.multiple_of(q * quarter, quarter), quarter)
        product = jnp.dot(x_v[rows, :], d_v[owner], preferred_element_type=f32)
        key = key_low[rows, :]
        low_acc[rows, :] = jnp.where(
            key == 2 * owner, product[:, :LANES],
            jnp.where(key == 2 * owner + 1, product[:, LANES:], low_acc[rows, :]),
        )

    def x_start(g):
        for i in range(1, SIDE):
            x_copy(i, g).start()

    x_local.wait()
    d_local.wait()

    @pl.loop(0, GROUP)
    def _(k):
        @pl.when(k < GROUP - 1)
        def _():
            d_arrival(k).wait_recv()
            d_forward(k, c).start()

        @pl.when(k + WINDOW < GROUP - 1)
        def _():
            d_copy(k + WINDOW).start()

        @pl.when(k == TOKENS_AT)
        def _():
            x_start(0)

        @pl.when(k == UP_AT)
        def _():
            for i in range(1, SIDE):
                u_copy(i).start()

        @pl.when(jnp.logical_and(k >= RING_AT[0], (k - RING_AT[0]) % RING_AT[1] == 0))
        def _():
            ring_event((k - RING_AT[0]) // RING_AT[1])

        @pl.when(k >= 1)
        def _():
            d_forward(k - 1, 1 - c).wait_recv()

        @pl.when(k < EARLY)
        def _():
            for q in range(SIDE):
                down_step(k, q)

    first_event = (GROUP - 1 - RING_AT[0]) // RING_AT[1] + 1

    lane_own = lax.broadcasted_iota(jnp.int32, (own, LANES), 1)

    def p_copy(i):
        return remote(p_send.at[(y + i) % SIDE], p_recv.at[i - 1], s_p.at[i], r_p.at[i], dp, y_peer(i))

    def q_copy(i):
        return remote(q_send, q_recv.at[i - 1], s_q.at[i], r_q.at[i], dp, x_peer(i))

    @pl.loop(1, SIDE + 1)
    def _(k):
        q = (y + k) % SIDE

        ring_event(first_event + k - 1)

        for i in range(EARLY, GROUP):
            down_step(i, q)

        packed = jnp.zeros((own, LANES), f32)
        for j in range(SIDE):
            v = low_acc[pl.ds(pl.multiple_of(q * quarter + j * own, own), own), :]
            v = v + pltpu.roll(v, 64, 1)
            v = v + pltpu.roll(v, 32, 1)
            packed = jnp.where((lane_own >> 5) == j, v, packed)
        p_send[q] = packed

        @pl.when(k < SIDE)
        def _():
            remote(p_send.at[q], p_recv.at[k - 1], s_p.at[k], r_p.at[k], dp, y_peer(k)).start()

    x_start(1)
    first_event += SIDE
    ring_event(first_event)
    for i in range(1, SIDE):
        p_copy(i).wait_recv()
    q_send[...] = (p_send[y] + p_recv[0]) + (p_recv[1] + p_recv[2])
    for i in range(1, SIDE):
        q_copy(i).start()
    x_start(2)
    x_start(3)
    for e in range(first_event + 1, 12):
        ring_event(e)
    u_local.wait()
    for i in range(1, SIDE):
        u_arrival(i).wait_recv()

    def u_forward(core):
        return remote(u_v.at[core], u_v.at[core], s_uf, r_uf, sib, me)

    u_forward(c).start()
    for i in range(1, SIDE):
        q_copy(i).wait_recv()
    low = ((q_send[...] + q_recv[0]) + (q_recv[1] + q_recv[2])).astype(bf16)
    low = (low.astype(f32) * ADAPTER_SCALE).astype(bf16)
    k_iota = lax.broadcasted_iota(jnp.int32, (LANES, LANES), 0)
    for j in range(SIDE):
        key = key_up[j * own:(j + 1) * own, :]
        for p in range(2):
            spread = (k_iota == 32 * j + 16 * p + (lane & 15)).astype(f32).astype(bf16)
            rows = jnp.dot(low, spread, preferred_element_type=f32)
            for g in range(SIDE):
                e_v[p, j * own:(j + 1) * own, g * LANES:(g + 1) * LANES] = jnp.where(
                    key == g, rows, 0.0
                ).astype(bf16)

    xq_local.wait()
    u_forward(1 - c).wait_recv()

    per_part = u_v.shape[2] // wide

    def block_at(t):
        return z_at(jnp.where(t % 2 == 1, -((t + 1) // 2), t // 2))

    def relay(t, n):
        to = jnp.where(t % 2 == 0, 1, SIDE - 1)
        return remote(relay_send.at[n], relay_recv.at[n], s_y.at[n], r_y.at[n], dp, x_peer(to))

    def o_copy(g, n):
        return remote(
            o_send.at[g - 1, n], o_recv.at[g - 1, n], s_o.at[g, n], r_o.at[g, n], dp, x_peer(TO[g])
        )

    for g in range(SIDE):
        for i in range(1, SIDE):
            x_arrival(i, g).wait_recv()
        rows = pl.ds(pl.multiple_of(own * ((x + TO[g]) % SIDE), own), own)

        @pl.loop(0, chips)
        def _(t):
            n = block_at(t)
            if g == 0:
                @pl.when(jnp.logical_or(t == 4, t == 5))
                def _():
                    ring_event(t + 8)

                for sub in range(2):
                    share(t, n, sub, 1 - c).wait_recv()
            p = n // per_part
            columns = pl.ds(pl.multiple_of((n % per_part) * wide, wide), wide)
            total = jnp.dot(xq[rows, :], w_v[n], preferred_element_type=f32) + jnp.dot(
                e_v[p, rows, :], u_v[p, :, columns], preferred_element_type=f32
            )
            if g == 0:
                relay_send[n] = total.astype(bf16)
                relay(t, n).start()
            elif g == SIDE - 1:
                acc_v[n] = total
            else:
                mine = t % 2 == g - 1

                @pl.when(mine)
                def _():
                    relay(t, n).wait_recv()
                    o_send[g - 1, n] = (total + relay_recv[n].astype(f32)).astype(bf16)

                @pl.when(jnp.logical_not(mine))
                def _():
                    o_send[g - 1, n] = total.astype(bf16)

                o_copy(g, n).start()

    @pl.loop(0, chips)
    def _(t):
        n = block_at(t)
        for g in range(1, SIDE - 1):
            o_copy(g, n).wait_recv()
        total = acc_v[n] + (o_recv[0, n].astype(f32) + o_recv[1, n].astype(f32))
        out_ref[:, pl.ds(pl.multiple_of(wide * n, wide), wide)] = total.astype(bf16)

    for i in range(1, SIDE):
        w_start(i).wait_send()
        for g in range(SIDE):
            x_copy(i, g).wait_send()
        u_copy(i).wait_send()
        p_copy(i).wait_send()
        q_copy(i).wait_send()

    @pl.when(c != to_core)
    def _():
        w_start(0).wait_send()

    u_forward(c).wait_send()

    @pl.loop(0, GROUP - 1)
    def _(k):
        d_copy(k).wait_send()
        d_forward(k, c).wait_send()

    @pl.loop(1, chips)
    def _(t):
        for sub in range(2):
            ring(t, z, sub, z).wait_send()

    @pl.loop(0, chips)
    def _(t):
        for sub in range(2):
            share(t, z, sub, c).wait_send()
        relay(t, t).wait_send()
        for g in range(1, SIDE - 1):
            o_copy(g, t).wait_send()


def local(tokens, frozen_weight, adapter_down_weight, adapter_up_weight, token_adapter_index):
    rows, depth = tokens.shape
    core_columns = frozen_weight.shape[1]
    devices = lax.axis_size("dp")
    chips = devices // 2
    columns = devices * core_columns
    present, rank, span = adapter_up_weight.shape[1:]
    quarter, own = rows // SIDE, rows // GROUP
    owner_columns = adapter_down_weight.shape[1]
    f32, bf16 = jnp.float32, jnp.bfloat16
    idx = token_adapter_index.reshape(rows // LANES, LANES)
    up = adapter_up_weight.reshape(2, present * rank, span)
    anywhere = pl.BlockSpec(memory_space=pl.ANY)
    vmem = pl.BlockSpec(memory_space=pltpu.VMEM)
    dma = pltpu.SemaphoreType.DMA
    return pl.pallas_call(
        body,
        out_shape=jax.ShapeDtypeStruct((own, columns), bf16),
        in_specs=[vmem, anywhere, anywhere, anywhere, anywhere],
        out_specs=vmem,
        scratch_shapes=[
            pltpu.VMEM((rows, depth), bf16),
            pltpu.VMEM((quarter, SIDE * depth), bf16),
            pltpu.VMEM((chips, SIDE * depth, 2 * core_columns), bf16),
            pltpu.VMEM((GROUP, depth, owner_columns), bf16),
            pltpu.VMEM((2, SIDE * present * rank, span), bf16),
            pltpu.VMEM((rows, LANES), f32),
            pltpu.VMEM((rows, LANES), jnp.int32),
            pltpu.VMEM((quarter, LANES), jnp.int32),
            pltpu.VMEM((SIDE, own, LANES), f32),
            pltpu.VMEM((SIDE - 1, own, LANES), f32),
            pltpu.VMEM((own, LANES), f32),
            pltpu.VMEM((SIDE - 1, own, LANES), f32),
            pltpu.VMEM((2, quarter, SIDE * present * rank), bf16),
            pltpu.VMEM((chips, own, 2 * core_columns), f32),
            pltpu.VMEM((2, chips, own, 2 * core_columns), bf16),
            pltpu.VMEM((2, chips, own, 2 * core_columns), bf16),
            pltpu.VMEM((chips, own, 2 * core_columns), bf16),
            pltpu.VMEM((chips, own, 2 * core_columns), bf16),
            dma((4,)),
            dma((GROUP,)), dma((GROUP,)), dma((GROUP,)), dma((GROUP,)),
            dma((4,)), dma((4,)), dma((SIDE, SIDE)), dma((SIDE, SIDE)), dma((SIDE,)), dma((SIDE,)),
            dma, dma,
            dma((chips, 2)), dma((chips, 2)), dma((chips, 2)), dma((chips, 2)),
            dma((SIDE,)), dma((SIDE,)), dma((SIDE,)), dma((SIDE,)),
            dma((SIDE, chips)), dma((SIDE, chips)), dma((chips,)), dma((chips,)),
        ],
        compiler_params=pltpu.CompilerParams(
            collective_id=0, has_side_effects=True, vmem_limit_bytes=60 << 20
        ),
        name="projections",
    )(idx, tokens, frozen_weight, adapter_down_weight, up)


def solution(mesh):
    placed = (P("dp", "mp"), P("mp", "dp"), P(None, "mp"), P(None, "mp", None, None), P("dp"))
    return jax.shard_map(
        local, mesh=mesh, in_specs=placed, out_specs=P(("dp", "mp"), None), check_vma=False
    )
```

```python
import jax
import jax.numpy as jnp
from jax import lax
from jax.experimental import pallas as pl
from jax.experimental.pallas import tpu as pltpu
from jax.sharding import PartitionSpec as P

SIDE = 4
GROUP = SIDE * SIDE
ADAPTER_SCALE = 2.0
LANES = 128
TO = (2, 1, 3, 0)
PEERS = (
    (0, 1), (0, 3), (0, 2), (2, 0), (2, 1), (2, 3), (2, 2),
    (1, 0), (3, 0), (1, 1), (3, 3), (1, 3), (3, 1), (1, 2), (3, 2),
)
ORDER_Y = sum(p[0] << (2 * k) for k, p in enumerate(PEERS))
ORDER_X = sum(p[1] << (2 * k) for k, p in enumerate(PEERS))
SHARED = (3, 7)
FIRST = 3
WINDOW = 6
Z_LAG = 8
TOKENS_AT = 12
UP_AT = 7
HALF_AT = 1
RING_AT = (3, 4, 9, 14)
TAIL_AT = (2,)
EXCHANGE_EVENTS = (0, 1, 0)
SEGMENTS = (
    (0, 0, 0, 7), (0, 1, 0, 4), (0, 2, 0, 4), (1, 0, 7, 8), (0, 1, 4, 8), (0, 2, 4, 8), (0, 3, 0, 8),
)
EVENTS = 7


def body(
    idx_ref, x_hbm, w_hbm, d_hbm, u_hbm, out_ref,
    x_v, xq, w_v, d_v, u_v, low_acc, key_low, key_up, p_send, p_recv, q_send, q_recv, p_own,
    e_v, acc_v, o_send, o_recv, relay_send, relay_recv,
    l_sem, s_d, r_d, s_f, r_f, s_z, r_z, s_w, r_w, s_x, r_x, s_u, r_u, s_v, r_v, s_uf, r_uf,
    s_r, r_r, s_s, r_s, s_p, r_p, s_q, r_q, s_o, r_o, s_y, r_y,
):
    f32, bf16 = jnp.float32, jnp.bfloat16
    depth = w_hbm.shape[0]
    quarter = xq.shape[0]
    own = out_ref.shape[0]
    wide = w_v.shape[2]
    chips = w_v.shape[0]
    half_d = depth // 2
    half_w = w_v.shape[1] // 2
    up_rows = u_hbm.shape[1]

    dp, me = lax.axis_index("dp"), lax.axis_index("mp")
    z, c = dp // 2, dp % 2
    y, x = me // SIDE, me % SIDE
    sib = 2 * z + 1 - c

    def z_at(step):
        return (z + step + chips) % chips

    def y_peer(step):
        return ((y + step) % SIDE) * SIDE + x

    def x_peer(step):
        return y * SIDE + (x + step) % SIDE

    def remote(src, dst, send_sem, recv_sem, d, m):
        return pltpu.make_async_remote_copy(
            src_ref=src, dst_ref=dst, send_sem=send_sem, recv_sem=recv_sem,
            device_id=(d, m), device_id_type=pl.DeviceIdType.MESH,
        )

    barrier = pltpu.get_barrier_semaphore()

    def greet(d, m):
        pl.semaphore_signal(barrier, inc=1, device_id=(d, m), device_id_type=pl.DeviceIdType.MESH)

    @pl.loop(1, GROUP)
    def _(i):
        greet(dp, (me + i) % GROUP)

    for i in range(1, SIDE):
        greet(sib, y_peer(i))
    greet(sib, me)
    greet(2 * z_at(1) + c, me)
    greet(2 * z_at(-1) + c, me)

    x_local = pltpu.make_async_copy(x_hbm, x_v, l_sem.at[0])
    x_local.start()
    d_local = pltpu.make_async_copy(d_hbm.at[pl.ds(depth * me, depth), :], d_v.at[me], l_sem.at[1])
    d_local.start()
    pl.semaphore_wait(barrier, GROUP - 1 + SIDE - 1 + 3)

    def d_peer(k, sign):
        dy, dx = (ORDER_Y >> (2 * k)) & 3, (ORDER_X >> (2 * k)) & 3
        return ((y + sign * dy + SIDE) % SIDE) * SIDE + (x + sign * dx + SIDE) % SIDE

    parity = z % 2
    quarter_d, eighth_d = half_d // 2, half_d // 4

    def d_rows(core, par):
        return half_d * core + quarter_d * par

    def d_part(k, core, shared):
        if shared:
            return pl.ds(d_rows(core, parity), quarter_d)
        return pl.ds(half_d * core, half_d)

    def d_copy(k, shared):
        peer = d_peer(k, 1)
        start, size = (d_rows(c, parity), quarter_d) if shared else (half_d * c, half_d)
        return remote(
            d_hbm.at[pl.ds(depth * peer + start, size), :], d_v.at[me, pl.ds(start, size), :],
            s_d.at[k], r_d.at[k], dp, peer,
        )

    def d_arrival(k, shared):
        block = d_v.at[d_peer(k, -1), d_part(k, c, shared), :]
        return remote(block, block, s_d.at[k], r_d.at[k], dp, me)

    def d_share(k, way, par):
        block = d_v.at[d_peer(k, -1), pl.ds(d_rows(c, par) + eighth_d * way, eighth_d), :]
        return remote(
            block, block, s_z.at[k, way], r_z.at[k, way], 2 * z_at(1 - 2 * way) + c, me
        )

    def d_forward(k, core, shared):
        block = d_v.at[d_peer(k, -1), d_part(k, core, shared), :]
        return remote(block, block, s_f.at[k, 0], r_f.at[k, 0], sib, me)

    def d_forward_other(k, core):
        block = d_v.at[d_peer(k, -1), pl.ds(d_rows(core, 1 - parity), quarter_d), :]
        return remote(block, block, s_f.at[k, 1], r_f.at[k, 1], sib, me)

    def is_shared(k):
        return jnp.logical_and(k >= SHARED[0], k < SHARED[1])

    def by_kind(k, low, high, do):
        @pl.when(jnp.logical_and(jnp.logical_and(k >= low, k < high), is_shared(k)))
        def _():
            do(True)

        @pl.when(
            jnp.logical_and(
                jnp.logical_and(k >= low, k < high), jnp.logical_not(is_shared(k))
            )
        )
        def _():
            do(False)

    for k in range(FIRST):
        d_copy(k, SHARED[0] <= k < SHARED[1]).start()

    to_core = y // 2
    w_slot = (y % 2) * 2 + c
    w_own = w_v.at[z, pl.ds(depth * y, depth), pl.ds(LANES * c, LANES)]

    def w_start(i):
        return remote(w_hbm, w_own, s_w.at[i], r_w.at[w_slot], 2 * z + to_core, y_peer(i))

    for i in range(1, SIDE):
        w_start(i).start()

    @pl.when(c == to_core)
    def _():
        pltpu.make_async_copy(w_hbm, w_own, r_w.at[w_slot]).start()

    @pl.when(c != to_core)
    def _():
        w_start(0).start()

    def x_block(row_y, column_y, g):
        to = (x + TO[g]) % SIDE
        return (
            x_hbm.at[pl.ds(quarter * row_y + own * to, own), :],
            xq.at[pl.ds(own * to, own), pl.ds(depth * column_y, depth)],
        )

    def x_copy(i, g):
        src, dst = x_block((y + i) % SIDE, y, g)
        return remote(src, dst, s_x.at[i, g], r_x.at[i, g], dp, y_peer(i))

    def x_arrival(i, g):
        _, dst = x_block(y, (y - i + SIDE) % SIDE, g)
        return remote(dst, dst, s_x.at[i, g], r_x.at[i, g], dp, me)

    xq_local = pltpu.make_async_copy(
        x_hbm.at[pl.ds(quarter * y, quarter), :], xq.at[:, pl.ds(depth * y, depth)], l_sem.at[2]
    )
    xq_local.start()

    half_u, quarter_u = up_rows // 2, up_rows // 4

    def u_part(block, par):
        return u_v.at[c, block, pl.ds(half_u * par, half_u), :]

    def u_copy(i):
        return remote(
            u_hbm.at[c, pl.ds(half_u * parity, half_u), :], u_part(y, parity),
            s_u.at[i], r_u.at[i], dp, y_peer(i),
        )

    def u_arrival(i):
        block = u_part((y - i + SIDE) % SIDE, parity)
        return remote(block, block, s_u.at[i], r_u.at[i], dp, me)

    def u_share(way, par):
        block = u_v.at[c, :, pl.ds(half_u * par + quarter_u * way, quarter_u), :]
        return remote(block, block, s_v.at[way], r_v.at[way], 2 * z_at(1 - 2 * way) + c, me)

    u_local = pltpu.make_async_copy(
        u_hbm.at[c, pl.ds(half_u * parity, half_u), :], u_part(y, parity), l_sem.at[3]
    )
    u_local.start()

    lane = lax.broadcasted_iota(jnp.int32, (LANES, LANES), 1)
    low_acc[...] = jnp.zeros_like(low_acc)

    def adapters(block):
        row = idx_ref[pl.ds(block, 1), :].astype(f32)
        return jnp.transpose(jnp.broadcast_to(row, (LANES, LANES))).astype(jnp.int32)

    @pl.loop(0, key_low.shape[0] // LANES)
    def _(b):
        a = adapters(b)
        key_low[pl.ds(pl.multiple_of(b * LANES, LANES), LANES), :] = jnp.where(
            (lane >> 5) == (a & 3), a >> 2, -1
        )

    @pl.loop(0, quarter // LANES)
    def _(b):
        a = adapters(y * (quarter // LANES) + b)
        owner = a >> 3
        mine = jnp.logical_and((owner & 3) == x, (lane >> 4) == (a & 7))
        key_up[pl.ds(pl.multiple_of(b * LANES, LANES), LANES), :] = jnp.where(mine, owner >> 2, -1)

    def piece(block, core, turn):
        return w_v.at[block, pl.ds(half_w * ((core + turn) % 2), half_w), :]

    def ring(j, turn, block):
        part = piece(block, c, turn)
        return remote(part, part, s_r.at[j, turn], r_r.at[j, turn], 2 * z_at(1 - 2 * c) + c, me)

    def share(t, turn, block, core):
        part = piece(block, core, turn)
        return remote(part, part, s_s.at[t, turn], r_s.at[t, turn], sib, me)

    def ring_start(turn):
        if turn == 0:
            for slot in range(4):
                block = w_v.at[
                    z, pl.ds(depth * (2 * c + slot // 2), depth), pl.ds(LANES * (slot % 2), LANES)
                ]
                remote(block, block, s_w.at[0], r_w.at[slot], dp, me).wait_recv()
            share(0, 0, z, c).start()
        else:
            share(0, 0, z, 1 - c).wait_recv()
        ring(1, turn, z).start()

    def ring_event(e):
        j, turn = e // 2 + 1, e % 2
        block = z_at(j * (2 * c - 1))
        ring(j, turn, block).wait_recv()

        @pl.when(e < EVENTS - 2)
        def _():
            ring(j + 1, turn, block).start()

        share(jnp.where(e < EVENTS - 1, 2 * j - 1 + c, EVENTS), turn, block, c).start()

    ring_start(0)
    for k in range(FIRST, WINDOW):
        d_copy(k, SHARED[0] <= k < SHARED[1]).start()

    def down_step(k, q):
        owner = jnp.where(k == 0, me, d_peer(jnp.maximum(k - 1, 0), -1))
        rows = pl.ds(pl.multiple_of(q * quarter, quarter), quarter)
        product = jnp.dot(x_v[rows, :], d_v[owner], preferred_element_type=f32)
        key = key_low[rows, :]
        low_acc[rows, :] = jnp.where(
            key == 2 * owner, product[:, :LANES],
            jnp.where(key == 2 * owner + 1, product[:, LANES:], low_acc[rows, :]),
        )

    def x_start(g):
        for i in range(1, SIDE):
            x_copy(i, g).start()

    x_local.wait()
    d_local.wait()

    @pl.loop(0, GROUP)
    def _(k):
        for e in range(len(RING_AT)):
            @pl.when(k == RING_AT[e])
            def _():
                ring_event(e)

        def arrive(shared):
            d_arrival(k, shared).wait_recv()
            d_forward(k, c, shared).start()
            if shared:
                for way in range(2):
                    d_share(k, way, parity).start()

        by_kind(k, 0, GROUP - 1, arrive)
        by_kind(k + WINDOW, WINDOW, GROUP - 1, lambda kind: d_copy(k + WINDOW, kind).start())

        @pl.when(k == HALF_AT)
        def _():
            ring_start(1)

        @pl.when(k == TOKENS_AT)
        def _():
            x_start(0)

        @pl.when(k == UP_AT)
        def _():
            for i in range(1, SIDE):
                u_copy(i).start()

        @pl.when(is_shared(k - Z_LAG))
        def _():
            for way in range(2):
                d_share(k - Z_LAG, way, 1 - parity).wait_recv()
            d_forward_other(k - Z_LAG, c).start()

        @pl.when(jnp.logical_not(is_shared(k - 1)))
        def _():
            @pl.when(k >= 1)
            def _():
                d_forward(k - 1, 1 - c, False).wait_recv()

            for q in range(SIDE):
                down_step(k, q)

    for k in range(*SHARED):
        d_forward(k, 1 - c, True).wait_recv()
        d_forward_other(k, 1 - c).wait_recv()
    first_event = len(RING_AT)

    lane_own = lax.broadcasted_iota(jnp.int32, (own, LANES), 1)

    def p_copy(i):
        return remote(p_send.at[(y + i) % SIDE], p_recv.at[i - 1], s_p.at[i], r_p.at[i], dp, y_peer(i))

    def q_copy(i):
        return remote(q_send, q_recv.at[i - 1], s_q.at[i], r_q.at[i], dp, x_peer(i))

    @pl.loop(1, SIDE + 1)
    def _(k):
        q = (y + k) % SIDE

        @pl.when(k == 1)
        def _():
            u_local.wait()
            for i in range(1, SIDE):
                u_arrival(i).wait_recv()
            for way in range(2):
                u_share(way, parity).start()

        for e in range(len(TAIL_AT)):
            @pl.when(k == TAIL_AT[e])
            def _():
                ring_event(first_event + e)

        for i in range(*SHARED):
            down_step(i + 1, q)

        packed = jnp.zeros((own, LANES), f32)
        for j in range(SIDE):
            v = low_acc[pl.ds(pl.multiple_of(q * quarter + j * own, own), own), :]
            v = v + pltpu.roll(v, 64, 1)
            v = v + pltpu.roll(v, 32, 1)
            packed = jnp.where((lane_own >> 5) == j, v, packed)
        p_send[q] = packed.astype(bf16)

        @pl.when(k == SIDE)
        def _():
            p_own[...] = packed

        @pl.when(k < SIDE)
        def _():
            remote(p_send.at[q], p_recv.at[k - 1], s_p.at[k], r_p.at[k], dp, y_peer(k)).start()

    x_start(1)
    first_event += len(TAIL_AT)
    def u_forward(core):
        return remote(u_v.at[core], u_v.at[core], s_uf, r_uf, sib, me)

    def ring_events(first, count):
        for e in range(first, min(first + count, EVENTS)):
            ring_event(e)
        return min(first + count, EVENTS)

    first_event = ring_events(first_event, EXCHANGE_EVENTS[0])
    for i in range(1, SIDE):
        p_copy(i).wait_recv()
    p_sum = p_own[...]
    for i in range(SIDE - 1):
        p_sum = p_sum + p_recv[i].astype(f32)
    p_own[...] = p_sum
    q_send[...] = p_sum.astype(bf16)
    for i in range(1, SIDE):
        q_copy(i).start()
    x_start(2)
    x_start(3)
    first_event = ring_events(first_event, EXCHANGE_EVENTS[1])
    for way in range(2):
        u_share(way, 1 - parity).wait_recv()
    u_forward(c).start()
    first_event = ring_events(first_event, EXCHANGE_EVENTS[2])
    for i in range(1, SIDE):
        q_copy(i).wait_recv()
    low = p_own[...]
    for i in range(SIDE - 1):
        low = low + q_recv[i].astype(f32)
    low = low.astype(bf16)
    low = (low.astype(f32) * ADAPTER_SCALE).astype(bf16)
    k_iota = lax.broadcasted_iota(jnp.int32, (LANES, LANES), 0)
    for j in range(SIDE):
        key = key_up[j * own:(j + 1) * own, :]
        for p in range(2):
            spread = (k_iota == 32 * j + 16 * p + (lane & 15)).astype(f32).astype(bf16)
            rows = jnp.dot(low, spread, preferred_element_type=f32)
            for g in range(SIDE):
                e_v[p, j * own:(j + 1) * own, g * LANES:(g + 1) * LANES] = jnp.where(
                    key == g, rows, 0.0
                ).astype(bf16)

    xq_local.wait()
    u_forward(1 - c).wait_recv()

    per_part = u_v.shape[3] // wide

    def block_at(t):
        return z_at(jnp.where(t % 2 == 1, -((t + 1) // 2), t // 2))

    def relay(t, n):
        to = jnp.where(t % 2 == 0, 1, SIDE - 1)
        return remote(relay_send.at[n], relay_recv.at[n], s_y.at[n], r_y.at[n], dp, x_peer(to))

    def o_copy(g, n):
        return remote(
            o_send.at[g - 1, n], o_recv.at[g - 1, n], s_o.at[g, n], r_o.at[g, n], dp, x_peer(TO[g])
        )

    seen = set()
    for events, g, first, end in SEGMENTS:
        if g not in seen:
            seen.add(g)
            for i in range(1, SIDE):
                x_arrival(i, g).wait_recv()
        first_event = ring_events(first_event, events)
        rows = pl.ds(pl.multiple_of(own * ((x + TO[g]) % SIDE), own), own)

        @pl.loop(first, end)
        def _(t):
            n = block_at(t)
            if g == 0:
                far = t == EVENTS

                @pl.when(jnp.logical_or(far, jnp.logical_and(t > 0, (t + 1) % 2 != c)))
                def _():
                    share(t, 0, n, 1 - c).wait_recv()

                    @pl.when(jnp.logical_not(far))
                    def _():
                        share(t, 1, n, 1 - c).wait_recv()
            p = n // per_part
            columns = pl.ds(pl.multiple_of((n % per_part) * wide, wide), wide)
            total = jnp.dot(xq[rows, :], w_v[n], preferred_element_type=f32) + jnp.dot(
                e_v[p, rows, :], u_v[p, :, :, columns].reshape(SIDE * up_rows, wide), preferred_element_type=f32
            )
            if g == 0:
                relay_send[n] = total.astype(bf16)
                relay(t, n).start()
            elif g == SIDE - 1:
                acc_v[n] = total
            else:
                mine = t % 2 == g - 1

                @pl.when(mine)
                def _():
                    relay(t, n).wait_recv()
                    o_send[g - 1, n] = (total + relay_recv[n].astype(f32)).astype(bf16)

                @pl.when(jnp.logical_not(mine))
                def _():
                    o_send[g - 1, n] = total.astype(bf16)

                o_copy(g, n).start()

    @pl.loop(0, chips)
    def _(t):
        n = block_at(t)
        for g in range(1, SIDE - 1):
            o_copy(g, n).wait_recv()
        total = acc_v[n] + (o_recv[0, n].astype(f32) + o_recv[1, n].astype(f32))
        out_ref[:, pl.ds(pl.multiple_of(wide * n, wide), wide)] = total.astype(bf16)

    for i in range(1, SIDE):
        w_start(i).wait_send()
        for g in range(SIDE):
            x_copy(i, g).wait_send()
        u_copy(i).wait_send()
        p_copy(i).wait_send()
        q_copy(i).wait_send()

    @pl.when(c != to_core)
    def _():
        w_start(0).wait_send()

    u_forward(c).wait_send()
    for way in range(2):
        u_share(way, parity).wait_send()

    @pl.loop(0, GROUP - 1)
    def _(k):
        def sent(shared):
            d_copy(k, shared).wait_send()
            d_forward(k, c, shared).wait_send()
            if shared:
                d_forward_other(k, c).wait_send()
                for way in range(2):
                    d_share(k, way, parity).wait_send()

        by_kind(k, 0, GROUP - 1, sent)

    for e in range(EVENTS):
        ring(e // 2 + 1, e % 2, z).wait_send()
        share(jnp.where(e < EVENTS - 1, 2 * (e // 2) + 1 + c, EVENTS), e % 2, z, c).wait_send()
    share(0, 0, z, c).wait_send()

    @pl.loop(0, chips)
    def _(t):
        relay(t, t).wait_send()
        for g in range(1, SIDE - 1):
            o_copy(g, t).wait_send()


def local(tokens, frozen_weight, adapter_down_weight, adapter_up_weight, token_adapter_index):
    rows, depth = tokens.shape
    core_columns = frozen_weight.shape[1]
    devices = lax.axis_size("dp")
    chips = devices // 2
    columns = devices * core_columns
    present, rank, span = adapter_up_weight.shape[1:]
    quarter, own = rows // SIDE, rows // GROUP
    owner_columns = adapter_down_weight.shape[1]
    f32, bf16 = jnp.float32, jnp.bfloat16
    idx = token_adapter_index.reshape(rows // LANES, LANES)
    up = adapter_up_weight.reshape(2, present * rank, span)
    anywhere = pl.BlockSpec(memory_space=pl.ANY)
    vmem = pl.BlockSpec(memory_space=pltpu.VMEM)
    dma = pltpu.SemaphoreType.DMA
    return pl.pallas_call(
        body,
        out_shape=jax.ShapeDtypeStruct((own, columns), bf16),
        in_specs=[vmem, anywhere, anywhere, anywhere, anywhere],
        out_specs=vmem,
        scratch_shapes=[
            pltpu.VMEM((rows, depth), bf16),
            pltpu.VMEM((quarter, SIDE * depth), bf16),
            pltpu.VMEM((chips, SIDE * depth, 2 * core_columns), bf16),
            pltpu.VMEM((GROUP, depth, owner_columns), bf16),
            pltpu.VMEM((2, SIDE, present * rank, span), bf16),
            pltpu.VMEM((rows, LANES), f32),
            pltpu.VMEM((rows, LANES), jnp.int32),
            pltpu.VMEM((quarter, LANES), jnp.int32),
            pltpu.VMEM((SIDE, own, LANES), bf16),
            pltpu.VMEM((SIDE - 1, own, LANES), bf16),
            pltpu.VMEM((own, LANES), bf16),
            pltpu.VMEM((SIDE - 1, own, LANES), bf16),
            pltpu.VMEM((own, LANES), f32),
            pltpu.VMEM((2, quarter, SIDE * present * rank), bf16),
            pltpu.VMEM((chips, own, 2 * core_columns), f32),
            pltpu.VMEM((2, chips, own, 2 * core_columns), bf16),
            pltpu.VMEM((2, chips, own, 2 * core_columns), bf16),
            pltpu.VMEM((chips, own, 2 * core_columns), bf16),
            pltpu.VMEM((chips, own, 2 * core_columns), bf16),
            dma((4,)),
            dma((GROUP,)), dma((GROUP,)), dma((GROUP, 2)), dma((GROUP, 2)), dma((GROUP, 2)), dma((GROUP, 2)),
            dma((4,)), dma((4,)), dma((SIDE, SIDE)), dma((SIDE, SIDE)), dma((SIDE,)), dma((SIDE,)), dma((2,)), dma((2,)),
            dma, dma,
            dma((chips, 2)), dma((chips, 2)), dma((chips, 2)), dma((chips, 2)),
            dma((SIDE,)), dma((SIDE,)), dma((SIDE,)), dma((SIDE,)),
            dma((SIDE, chips)), dma((SIDE, chips)), dma((chips,)), dma((chips,)),
        ],
        compiler_params=pltpu.CompilerParams(
            collective_id=0, has_side_effects=True, vmem_limit_bytes=60 << 20
        ),
        name="projections",
    )(idx, tokens, frozen_weight, adapter_down_weight, up)


def solution(mesh):
    placed = (P("dp", "mp"), P("mp", "dp"), P(None, "mp"), P(None, "mp", None, None), P("dp"))
    return jax.shard_map(
        local, mesh=mesh, in_specs=placed, out_specs=P(("dp", "mp"), None), check_vma=False
    )
```

```python
import jax
import jax.numpy as jnp
from jax import lax
from jax.experimental import pallas as pl
from jax.experimental.pallas import tpu as pltpu
from jax.sharding import PartitionSpec as P

SIDE = 4
GROUP = SIDE * SIDE
ADAPTER_SCALE = 2.0
LANES = 128
TO = (2, 1, 3, 0)
PEERS = (
    (0, 1), (0, 3), (0, 2), (2, 0), (2, 1), (2, 3), (2, 2),
    (1, 0), (3, 0), (1, 1), (3, 3), (1, 3), (3, 1), (1, 2), (3, 2),
)
ORDER_Y = sum(p[0] << (2 * k) for k, p in enumerate(PEERS))
ORDER_X = sum(p[1] << (2 * k) for k, p in enumerate(PEERS))
SHARED = (3, 7)
FIRST = 3
WINDOW = 6
Z_LAG = 8
TOKENS_AT = 12
UP_AT = 7
AFTER_DOWN = (1, 2)
HALF_AT = 1
RING_AT = (3, 9, 13)
TAIL_AT = (1,)
EXCHANGE_EVENTS = (1, 0, 0)
SEGMENTS = (
    (0, 0, 0, 5), (1, 0, 5, 7), (0, 1, 0, 4), (0, 2, 0, 4), (1, 0, 7, 8), (0, 1, 4, 8), (0, 2, 4, 8),
    (0, 3, 0, 8),
)
EVENTS = 7


def body(
    idx_ref, x_hbm, w_hbm, d_hbm, u_hbm, out_ref,
    x_v, xq, w_v, d_v, u_v, low_acc, key_low, key_up, p_send, p_recv, q_send, q_recv, p_own,
    e_v, acc_v, o_send, o_recv, relay_send, relay_recv,
    l_sem, s_d, r_d, s_f, r_f, s_z, r_z, s_w, r_w, s_x, r_x, s_u, r_u, s_v, r_v, s_uf, r_uf,
    s_r, r_r, s_s, r_s, s_p, r_p, s_q, r_q, s_o, r_o, s_y, r_y,
):
    f32, bf16 = jnp.float32, jnp.bfloat16
    depth = w_hbm.shape[0]
    quarter = xq.shape[0]
    own = out_ref.shape[0]
    wide = w_v.shape[2]
    chips = w_v.shape[0]
    half_d = depth // 2
    half_w = w_v.shape[1] // 2
    up_rows = u_hbm.shape[1]

    dp, me = lax.axis_index("dp"), lax.axis_index("mp")
    z, c = dp // 2, dp % 2
    y, x = me // SIDE, me % SIDE
    sib = 2 * z + 1 - c

    def z_at(step):
        return (z + step + chips) % chips

    def y_peer(step):
        return ((y + step) % SIDE) * SIDE + x

    def x_peer(step):
        return y * SIDE + (x + step) % SIDE

    def remote(src, dst, send_sem, recv_sem, d, m):
        return pltpu.make_async_remote_copy(
            src_ref=src, dst_ref=dst, send_sem=send_sem, recv_sem=recv_sem,
            device_id=(d, m), device_id_type=pl.DeviceIdType.MESH,
        )

    barrier = pltpu.get_barrier_semaphore()

    def greet(d, m):
        pl.semaphore_signal(barrier, inc=1, device_id=(d, m), device_id_type=pl.DeviceIdType.MESH)

    @pl.loop(1, GROUP)
    def _(i):
        greet(dp, (me + i) % GROUP)

    for i in range(1, SIDE):
        greet(sib, y_peer(i))
    greet(sib, me)
    greet(2 * z_at(1) + c, me)
    greet(2 * z_at(-1) + c, me)

    x_local = pltpu.make_async_copy(x_hbm, x_v, l_sem.at[0])
    x_local.start()
    d_local = pltpu.make_async_copy(d_hbm.at[pl.ds(depth * me, depth), :], d_v.at[me], l_sem.at[1])
    d_local.start()
    pl.semaphore_wait(barrier, GROUP - 1 + SIDE - 1 + 3)

    def d_peer(k, sign):
        dy, dx = (ORDER_Y >> (2 * k)) & 3, (ORDER_X >> (2 * k)) & 3
        return ((y + sign * dy + SIDE) % SIDE) * SIDE + (x + sign * dx + SIDE) % SIDE

    parity = z % 2
    quarter_d, eighth_d = half_d // 2, half_d // 4

    def d_rows(core, par):
        return half_d * core + quarter_d * par

    def d_part(k, core, shared):
        if shared:
            return pl.ds(d_rows(core, parity), quarter_d)
        return pl.ds(half_d * core, half_d)

    def d_copy(k, shared):
        peer = d_peer(k, 1)
        start, size = (d_rows(c, parity), quarter_d) if shared else (half_d * c, half_d)
        return remote(
            d_hbm.at[pl.ds(depth * peer + start, size), :], d_v.at[me, pl.ds(start, size), :],
            s_d.at[k], r_d.at[k], dp, peer,
        )

    def d_arrival(k, shared):
        block = d_v.at[d_peer(k, -1), d_part(k, c, shared), :]
        return remote(block, block, s_d.at[k], r_d.at[k], dp, me)

    def d_share(k, way, par):
        block = d_v.at[d_peer(k, -1), pl.ds(d_rows(c, par) + eighth_d * way, eighth_d), :]
        return remote(
            block, block, s_z.at[k, way], r_z.at[k, way], 2 * z_at(1 - 2 * way) + c, me
        )

    def d_forward(k, core, shared):
        block = d_v.at[d_peer(k, -1), d_part(k, core, shared), :]
        return remote(block, block, s_f.at[k, 0], r_f.at[k, 0], sib, me)

    def d_forward_other(k, core):
        block = d_v.at[d_peer(k, -1), pl.ds(d_rows(core, 1 - parity), quarter_d), :]
        return remote(block, block, s_f.at[k, 1], r_f.at[k, 1], sib, me)

    def is_shared(k):
        return jnp.logical_and(k >= SHARED[0], k < SHARED[1])

    def by_kind(k, low, high, do):
        @pl.when(jnp.logical_and(jnp.logical_and(k >= low, k < high), is_shared(k)))
        def _():
            do(True)

        @pl.when(
            jnp.logical_and(
                jnp.logical_and(k >= low, k < high), jnp.logical_not(is_shared(k))
            )
        )
        def _():
            do(False)

    for k in range(FIRST):
        d_copy(k, SHARED[0] <= k < SHARED[1]).start()

    to_core = y // 2
    w_slot = (y % 2) * 2 + c
    w_own = w_v.at[z, pl.ds(depth * y, depth), pl.ds(LANES * c, LANES)]

    def w_start(i):
        return remote(w_hbm, w_own, s_w.at[i], r_w.at[w_slot], 2 * z + to_core, y_peer(i))

    for i in range(1, SIDE):
        w_start(i).start()

    @pl.when(c == to_core)
    def _():
        pltpu.make_async_copy(w_hbm, w_own, r_w.at[w_slot]).start()

    @pl.when(c != to_core)
    def _():
        w_start(0).start()

    def x_block(row_y, column_y, g):
        to = (x + TO[g]) % SIDE
        return (
            x_hbm.at[pl.ds(quarter * row_y + own * to, own), :],
            xq.at[pl.ds(own * to, own), pl.ds(depth * column_y, depth)],
        )

    def x_copy(i, g):
        src, dst = x_block((y + i) % SIDE, y, g)
        return remote(src, dst, s_x.at[i, g], r_x.at[i, g], dp, y_peer(i))

    def x_arrival(i, g):
        _, dst = x_block(y, (y - i + SIDE) % SIDE, g)
        return remote(dst, dst, s_x.at[i, g], r_x.at[i, g], dp, me)

    xq_local = pltpu.make_async_copy(
        x_hbm.at[pl.ds(quarter * y, quarter), :], xq.at[:, pl.ds(depth * y, depth)], l_sem.at[2]
    )
    xq_local.start()

    half_u, quarter_u = up_rows // 2, up_rows // 4

    def u_part(block, par):
        return u_v.at[c, block, pl.ds(half_u * par, half_u), :]

    def u_copy(i):
        return remote(
            u_hbm.at[c, pl.ds(half_u * parity, half_u), :], u_part(y, parity),
            s_u.at[i], r_u.at[i], dp, y_peer(i),
        )

    def u_arrival(i):
        block = u_part((y - i + SIDE) % SIDE, parity)
        return remote(block, block, s_u.at[i], r_u.at[i], dp, me)

    def u_share(way, par):
        block = u_v.at[c, :, pl.ds(half_u * par + quarter_u * way, quarter_u), :]
        return remote(block, block, s_v.at[way], r_v.at[way], 2 * z_at(1 - 2 * way) + c, me)

    u_local = pltpu.make_async_copy(
        u_hbm.at[c, pl.ds(half_u * parity, half_u), :], u_part(y, parity), l_sem.at[3]
    )
    u_local.start()

    lane = lax.broadcasted_iota(jnp.int32, (LANES, LANES), 1)
    low_acc[...] = jnp.zeros_like(low_acc)

    def adapters(block):
        row = idx_ref[pl.ds(block, 1), :].astype(f32)
        return jnp.transpose(jnp.broadcast_to(row, (LANES, LANES))).astype(jnp.int32)

    @pl.loop(0, key_low.shape[0] // LANES)
    def _(b):
        a = adapters(b)
        key_low[pl.ds(pl.multiple_of(b * LANES, LANES), LANES), :] = jnp.where(
            (lane >> 5) == (a & 3), a >> 2, -1
        )

    @pl.loop(0, quarter // LANES)
    def _(b):
        a = adapters(y * (quarter // LANES) + b)
        owner = a >> 3
        mine = jnp.logical_and((owner & 3) == x, (lane >> 4) == (a & 7))
        key_up[pl.ds(pl.multiple_of(b * LANES, LANES), LANES), :] = jnp.where(mine, owner >> 2, -1)

    def piece(block, core, turn):
        return w_v.at[block, pl.ds(half_w * ((core + turn) % 2), half_w), :]

    def ring(j, turn, block):
        part = piece(block, c, turn)
        return remote(part, part, s_r.at[j, turn], r_r.at[j, turn], 2 * z_at(1 - 2 * c) + c, me)

    def share(t, turn, block, core):
        part = piece(block, core, turn)
        return remote(part, part, s_s.at[t, turn], r_s.at[t, turn], sib, me)

    def ring_start(turn):
        if turn == 0:
            for slot in range(4):
                block = w_v.at[
                    z, pl.ds(depth * (2 * c + slot // 2), depth), pl.ds(LANES * (slot % 2), LANES)
                ]
                remote(block, block, s_w.at[0], r_w.at[slot], dp, me).wait_recv()
            share(0, 0, z, c).start()
        else:
            share(0, 0, z, 1 - c).wait_recv()
        ring(1, turn, z).start()

    def ring_event(e):
        j, turn = e // 2 + 1, e % 2
        block = z_at(j * (2 * c - 1))
        ring(j, turn, block).wait_recv()

        @pl.when(e < EVENTS - 2)
        def _():
            ring(j + 1, turn, block).start()

        share(jnp.where(e < EVENTS - 1, 2 * j - 1 + c, EVENTS), turn, block, c).start()

    ring_start(0)
    for k in range(FIRST, WINDOW):
        d_copy(k, SHARED[0] <= k < SHARED[1]).start()

    def down_step(k, q):
        owner = jnp.where(k == 0, me, d_peer(jnp.maximum(k - 1, 0), -1))
        rows = pl.ds(pl.multiple_of(q * quarter, quarter), quarter)
        product = jnp.dot(x_v[rows, :], d_v[owner], preferred_element_type=f32)
        key = key_low[rows, :]
        low_acc[rows, :] = jnp.where(
            key == 2 * owner, product[:, :LANES],
            jnp.where(key == 2 * owner + 1, product[:, LANES:], low_acc[rows, :]),
        )

    def x_start(g):
        for i in range(1, SIDE):
            x_copy(i, g).start()

    x_local.wait()
    d_local.wait()

    @pl.loop(0, GROUP)
    def _(k):
        for e in range(len(RING_AT)):
            @pl.when(k == RING_AT[e])
            def _():
                ring_event(e)

        def arrive(shared):
            d_arrival(k, shared).wait_recv()
            d_forward(k, c, shared).start()
            if shared:
                for way in range(2):
                    d_share(k, way, parity).start()

        by_kind(k, 0, GROUP - 1, arrive)
        by_kind(k + WINDOW, WINDOW, GROUP - 1, lambda kind: d_copy(k + WINDOW, kind).start())

        @pl.when(k == HALF_AT)
        def _():
            ring_start(1)

        @pl.when(k == TOKENS_AT)
        def _():
            x_start(0)

        @pl.when(k == UP_AT)
        def _():
            for i in range(1, SIDE):
                u_copy(i).start()

        @pl.when(is_shared(k - Z_LAG))
        def _():
            for way in range(2):
                d_share(k - Z_LAG, way, 1 - parity).wait_recv()
            d_forward_other(k - Z_LAG, c).start()

        @pl.when(jnp.logical_not(is_shared(k - 1)))
        def _():
            @pl.when(k >= 1)
            def _():
                d_forward(k - 1, 1 - c, False).wait_recv()

            for q in range(SIDE):
                down_step(k, q)

    for k in range(*SHARED):
        d_forward(k, 1 - c, True).wait_recv()
        d_forward_other(k, 1 - c).wait_recv()
    first_event = len(RING_AT)

    lane_own = lax.broadcasted_iota(jnp.int32, (own, LANES), 1)

    def p_copy(i):
        return remote(p_send.at[(y + i) % SIDE], p_recv.at[i - 1], s_p.at[i], r_p.at[i], dp, y_peer(i))

    def q_copy(i):
        return remote(q_send, q_recv.at[i - 1], s_q.at[i], r_q.at[i], dp, x_peer(i))

    @pl.loop(1, SIDE + 1)
    def _(k):
        q = (y + k) % SIDE

        @pl.when(k == 1)
        def _():
            u_local.wait()
            for i in range(1, SIDE):
                u_arrival(i).wait_recv()
            for way in range(2):
                u_share(way, parity).start()

        for e in range(len(TAIL_AT)):
            @pl.when(k == TAIL_AT[e])
            def _():
                ring_event(first_event + e)

        for i in range(*SHARED):
            down_step(i + 1, q)

        packed = jnp.zeros((own, LANES), f32)
        for j in range(SIDE):
            v = low_acc[pl.ds(pl.multiple_of(q * quarter + j * own, own), own), :]
            v = v + pltpu.roll(v, 64, 1)
            v = v + pltpu.roll(v, 32, 1)
            packed = jnp.where((lane_own >> 5) == j, v, packed)
        p_send[q] = packed.astype(bf16)

        @pl.when(k == SIDE)
        def _():
            p_own[...] = packed

        @pl.when(k < SIDE)
        def _():
            remote(p_send.at[q], p_recv.at[k - 1], s_p.at[k], r_p.at[k], dp, y_peer(k)).start()

    for g in AFTER_DOWN:
        x_start(g)
    first_event += len(TAIL_AT)
    def u_forward(core):
        return remote(u_v.at[core], u_v.at[core], s_uf, r_uf, sib, me)

    def ring_events(first, count):
        for e in range(first, min(first + count, EVENTS)):
            ring_event(e)
        return min(first + count, EVENTS)

    first_event = ring_events(first_event, EXCHANGE_EVENTS[0])
    for i in range(1, SIDE):
        p_copy(i).wait_recv()
    p_sum = p_own[...]
    for i in range(SIDE - 1):
        p_sum = p_sum + p_recv[i].astype(f32)
    p_own[...] = p_sum
    q_send[...] = p_sum.astype(bf16)
    for i in range(1, SIDE):
        q_copy(i).start()
    for g in range(1 + len(AFTER_DOWN), SIDE):
        x_start(g)
    first_event = ring_events(first_event, EXCHANGE_EVENTS[1])
    for way in range(2):
        u_share(way, 1 - parity).wait_recv()
    u_forward(c).start()
    first_event = ring_events(first_event, EXCHANGE_EVENTS[2])
    for i in range(1, SIDE):
        q_copy(i).wait_recv()
    low = p_own[...]
    for i in range(SIDE - 1):
        low = low + q_recv[i].astype(f32)
    low = low.astype(bf16)
    low = (low.astype(f32) * ADAPTER_SCALE).astype(bf16)
    k_iota = lax.broadcasted_iota(jnp.int32, (LANES, LANES), 0)
    for j in range(SIDE):
        key = key_up[j * own:(j + 1) * own, :]
        for p in range(2):
            spread = (k_iota == 32 * j + 16 * p + (lane & 15)).astype(f32).astype(bf16)
            rows = jnp.dot(low, spread, preferred_element_type=f32)
            for g in range(SIDE):
                e_v[p, j * own:(j + 1) * own, g * LANES:(g + 1) * LANES] = jnp.where(
                    key == g, rows, 0.0
                ).astype(bf16)

    xq_local.wait()
    u_forward(1 - c).wait_recv()

    per_part = u_v.shape[3] // wide

    def block_at(t):
        return z_at(jnp.where(t % 2 == 1, -((t + 1) // 2), t // 2))

    def relay(t, n):
        to = jnp.where(t % 2 == 0, 1, SIDE - 1)
        return remote(relay_send.at[n], relay_recv.at[n], s_y.at[n], r_y.at[n], dp, x_peer(to))

    def o_copy(g, n):
        return remote(
            o_send.at[g - 1, n], o_recv.at[g - 1, n], s_o.at[g, n], r_o.at[g, n], dp, x_peer(TO[g])
        )

    seen = set()
    for events, g, first, end in SEGMENTS:
        if g not in seen:
            seen.add(g)
            for i in range(1, SIDE):
                x_arrival(i, g).wait_recv()
        first_event = ring_events(first_event, events)
        rows = pl.ds(pl.multiple_of(own * ((x + TO[g]) % SIDE), own), own)

        @pl.loop(first, end)
        def _(t):
            n = block_at(t)
            if g == 0:
                far = t == EVENTS

                @pl.when(jnp.logical_or(far, jnp.logical_and(t > 0, (t + 1) % 2 != c)))
                def _():
                    share(t, 0, n, 1 - c).wait_recv()

                    @pl.when(jnp.logical_not(far))
                    def _():
                        share(t, 1, n, 1 - c).wait_recv()
            p = n // per_part
            columns = pl.ds(pl.multiple_of((n % per_part) * wide, wide), wide)
            total = jnp.dot(xq[rows, :], w_v[n], preferred_element_type=f32) + jnp.dot(
                e_v[p, rows, :], u_v[p, :, :, columns].reshape(SIDE * up_rows, wide), preferred_element_type=f32
            )
            if g == 0:
                relay_send[n] = total.astype(bf16)
                relay(t, n).start()
            elif g == SIDE - 1:
                acc_v[n] = total
            else:
                mine = t % 2 == g - 1

                @pl.when(mine)
                def _():
                    relay(t, n).wait_recv()
                    o_send[g - 1, n] = (total + relay_recv[n].astype(f32)).astype(bf16)

                @pl.when(jnp.logical_not(mine))
                def _():
                    o_send[g - 1, n] = total.astype(bf16)

                o_copy(g, n).start()

    @pl.loop(0, chips)
    def _(t):
        n = block_at(t)
        for g in range(1, SIDE - 1):
            o_copy(g, n).wait_recv()
        total = acc_v[n] + (o_recv[0, n].astype(f32) + o_recv[1, n].astype(f32))
        out_ref[:, pl.ds(pl.multiple_of(wide * n, wide), wide)] = total.astype(bf16)

    for i in range(1, SIDE):
        w_start(i).wait_send()
        for g in range(SIDE):
            x_copy(i, g).wait_send()
        u_copy(i).wait_send()
        p_copy(i).wait_send()
        q_copy(i).wait_send()

    @pl.when(c != to_core)
    def _():
        w_start(0).wait_send()

    u_forward(c).wait_send()
    for way in range(2):
        u_share(way, parity).wait_send()

    @pl.loop(0, GROUP - 1)
    def _(k):
        def sent(shared):
            d_copy(k, shared).wait_send()
            d_forward(k, c, shared).wait_send()
            if shared:
                d_forward_other(k, c).wait_send()
                for way in range(2):
                    d_share(k, way, parity).wait_send()

        by_kind(k, 0, GROUP - 1, sent)

    for e in range(EVENTS):
        ring(e // 2 + 1, e % 2, z).wait_send()
        share(jnp.where(e < EVENTS - 1, 2 * (e // 2) + 1 + c, EVENTS), e % 2, z, c).wait_send()
    share(0, 0, z, c).wait_send()

    @pl.loop(0, chips)
    def _(t):
        relay(t, t).wait_send()
        for g in range(1, SIDE - 1):
            o_copy(g, t).wait_send()


def local(tokens, frozen_weight, adapter_down_weight, adapter_up_weight, token_adapter_index):
    rows, depth = tokens.shape
    core_columns = frozen_weight.shape[1]
    devices = lax.axis_size("dp")
    chips = devices // 2
    columns = devices * core_columns
    present, rank, span = adapter_up_weight.shape[1:]
    quarter, own = rows // SIDE, rows // GROUP
    owner_columns = adapter_down_weight.shape[1]
    f32, bf16 = jnp.float32, jnp.bfloat16
    idx = token_adapter_index.reshape(rows // LANES, LANES)
    up = adapter_up_weight.reshape(2, present * rank, span)
    anywhere = pl.BlockSpec(memory_space=pl.ANY)
    vmem = pl.BlockSpec(memory_space=pltpu.VMEM)
    dma = pltpu.SemaphoreType.DMA
    return pl.pallas_call(
        body,
        out_shape=jax.ShapeDtypeStruct((own, columns), bf16),
        in_specs=[vmem, anywhere, anywhere, anywhere, anywhere],
        out_specs=vmem,
        scratch_shapes=[
            pltpu.VMEM((rows, depth), bf16),
            pltpu.VMEM((quarter, SIDE * depth), bf16),
            pltpu.VMEM((chips, SIDE * depth, 2 * core_columns), bf16),
            pltpu.VMEM((GROUP, depth, owner_columns), bf16),
            pltpu.VMEM((2, SIDE, present * rank, span), bf16),
            pltpu.VMEM((rows, LANES), f32),
            pltpu.VMEM((rows, LANES), jnp.int32),
            pltpu.VMEM((quarter, LANES), jnp.int32),
            pltpu.VMEM((SIDE, own, LANES), bf16),
            pltpu.VMEM((SIDE - 1, own, LANES), bf16),
            pltpu.VMEM((own, LANES), bf16),
            pltpu.VMEM((SIDE - 1, own, LANES), bf16),
            pltpu.VMEM((own, LANES), f32),
            pltpu.VMEM((2, quarter, SIDE * present * rank), bf16),
            pltpu.VMEM((chips, own, 2 * core_columns), f32),
            pltpu.VMEM((2, chips, own, 2 * core_columns), bf16),
            pltpu.VMEM((2, chips, own, 2 * core_columns), bf16),
            pltpu.VMEM((chips, own, 2 * core_columns), bf16),
            pltpu.VMEM((chips, own, 2 * core_columns), bf16),
            dma((4,)),
            dma((GROUP,)), dma((GROUP,)), dma((GROUP, 2)), dma((GROUP, 2)), dma((GROUP, 2)), dma((GROUP, 2)),
            dma((4,)), dma((4,)), dma((SIDE, SIDE)), dma((SIDE, SIDE)), dma((SIDE,)), dma((SIDE,)), dma((2,)), dma((2,)),
            dma, dma,
            dma((chips, 2)), dma((chips, 2)), dma((chips, 2)), dma((chips, 2)),
            dma((SIDE,)), dma((SIDE,)), dma((SIDE,)), dma((SIDE,)),
            dma((SIDE, chips)), dma((SIDE, chips)), dma((chips,)), dma((chips,)),
        ],
        compiler_params=pltpu.CompilerParams(
            collective_id=0, has_side_effects=True, vmem_limit_bytes=60 << 20
        ),
        name="projections",
    )(idx, tokens, frozen_weight, adapter_down_weight, up)


def solution(mesh):
    placed = (P("dp", "mp"), P("mp", "dp"), P(None, "mp"), P(None, "mp", None, None), P("dp"))
    return jax.shard_map(
        local, mesh=mesh, in_specs=placed, out_specs=P(("dp", "mp"), None), check_vma=False
    )
```

```python
import jax
import jax.numpy as jnp
from jax import lax
from jax.experimental import pallas as pl
from jax.experimental.pallas import tpu as pltpu
from jax.sharding import PartitionSpec as P

SIDE = 4
GROUP = SIDE * SIDE
ADAPTER_SCALE = 2.0
LANES = 128
TO = (2, 1, 3, 0)
PEERS = (
    (0, 1), (0, 3), (0, 2), (2, 0), (2, 1), (2, 3), (2, 2),
    (1, 0), (3, 0), (1, 1), (3, 3), (1, 3), (3, 1), (1, 2), (3, 2),
)
ORDER_Y = sum(p[0] << (2 * k) for k, p in enumerate(PEERS))
ORDER_X = sum(p[1] << (2 * k) for k, p in enumerate(PEERS))
SHARED = (3, 7)
FIRST = 3
WINDOW = 6
Z_LAG = 8
TOKENS_AT = 10
UP_AT = 7
AFTER_DOWN = (1, 2)
HALF_AT = 1
RING_AT = (3, 9, 13)
TAIL_AT = (1,)
EXCHANGE_EVENTS = (1, 0, 0)
SEGMENTS = (
    (0, 0, 0, 5), (1, 0, 5, 7), (0, 1, 0, 4), (0, 2, 0, 4), (1, 0, 7, 8), (0, 1, 4, 8), (0, 2, 4, 8),
    (0, 3, 0, 8),
)
EVENTS = 7


def body(
    idx_ref, x_hbm, w_hbm, d_hbm, u_hbm, out_ref,
    x_v, xq, w_v, d_v, u_v, low_acc, key_low, key_up, p_send, p_recv, q_send, q_recv, p_own,
    e_v, acc_v, o_send, o_recv, relay_send, relay_recv,
    l_sem, s_d, r_d, s_f, r_f, s_z, r_z, s_w, r_w, s_x, r_x, s_u, r_u, s_v, r_v, s_uf, r_uf,
    s_r, r_r, s_s, r_s, s_p, r_p, s_q, r_q, s_o, r_o, s_y, r_y,
):
    f32, bf16 = jnp.float32, jnp.bfloat16
    depth = w_hbm.shape[0]
    quarter = xq.shape[0]
    own = out_ref.shape[0]
    wide = w_v.shape[2]
    chips = w_v.shape[0]
    half_d = depth // 2
    half_w = w_v.shape[1] // 2
    up_rows = u_hbm.shape[1]

    dp, me = lax.axis_index("dp"), lax.axis_index("mp")
    z, c = dp // 2, dp % 2
    y, x = me // SIDE, me % SIDE
    sib = 2 * z + 1 - c

    def z_at(step):
        return (z + step + chips) % chips

    def y_peer(step):
        return ((y + step) % SIDE) * SIDE + x

    def x_peer(step):
        return y * SIDE + (x + step) % SIDE

    def remote(src, dst, send_sem, recv_sem, d, m):
        return pltpu.make_async_remote_copy(
            src_ref=src, dst_ref=dst, send_sem=send_sem, recv_sem=recv_sem,
            device_id=(d, m), device_id_type=pl.DeviceIdType.MESH,
        )

    barrier = pltpu.get_barrier_semaphore()

    def greet(d, m):
        pl.semaphore_signal(barrier, inc=1, device_id=(d, m), device_id_type=pl.DeviceIdType.MESH)

    @pl.loop(1, GROUP)
    def _(i):
        greet(dp, (me + i) % GROUP)

    for i in range(1, SIDE):
        greet(sib, y_peer(i))
    greet(sib, me)
    greet(2 * z_at(1) + c, me)
    greet(2 * z_at(-1) + c, me)

    x_local = pltpu.make_async_copy(x_hbm, x_v, l_sem.at[0])
    x_local.start()
    d_local = pltpu.make_async_copy(d_hbm.at[pl.ds(depth * me, depth), :], d_v.at[me], l_sem.at[1])
    d_local.start()
    pl.semaphore_wait(barrier, GROUP - 1 + SIDE - 1 + 3)

    def d_peer(k, sign):
        dy, dx = (ORDER_Y >> (2 * k)) & 3, (ORDER_X >> (2 * k)) & 3
        return ((y + sign * dy + SIDE) % SIDE) * SIDE + (x + sign * dx + SIDE) % SIDE

    parity = z % 2
    quarter_d, eighth_d = half_d // 2, half_d // 4

    def d_rows(core, par):
        return half_d * core + quarter_d * par

    def d_part(k, core, shared):
        if shared:
            return pl.ds(d_rows(core, parity), quarter_d)
        return pl.ds(half_d * core, half_d)

    def d_copy(k, shared):
        peer = d_peer(k, 1)
        start, size = (d_rows(c, parity), quarter_d) if shared else (half_d * c, half_d)
        return remote(
            d_hbm.at[pl.ds(depth * peer + start, size), :], d_v.at[me, pl.ds(start, size), :],
            s_d.at[k], r_d.at[k], dp, peer,
        )

    def d_arrival(k, shared):
        block = d_v.at[d_peer(k, -1), d_part(k, c, shared), :]
        return remote(block, block, s_d.at[k], r_d.at[k], dp, me)

    def d_share(k, way, par):
        block = d_v.at[d_peer(k, -1), pl.ds(d_rows(c, par) + eighth_d * way, eighth_d), :]
        return remote(
            block, block, s_z.at[k, way], r_z.at[k, way], 2 * z_at(1 - 2 * way) + c, me
        )

    def d_forward(k, core, shared):
        block = d_v.at[d_peer(k, -1), d_part(k, core, shared), :]
        return remote(block, block, s_f.at[k, 0], r_f.at[k, 0], sib, me)

    def d_forward_other(k, core):
        block = d_v.at[d_peer(k, -1), pl.ds(d_rows(core, 1 - parity), quarter_d), :]
        return remote(block, block, s_f.at[k, 1], r_f.at[k, 1], sib, me)

    def is_shared(k):
        return jnp.logical_and(k >= SHARED[0], k < SHARED[1])

    def by_kind(k, low, high, do):
        @pl.when(jnp.logical_and(jnp.logical_and(k >= low, k < high), is_shared(k)))
        def _():
            do(True)

        @pl.when(
            jnp.logical_and(
                jnp.logical_and(k >= low, k < high), jnp.logical_not(is_shared(k))
            )
        )
        def _():
            do(False)

    for k in range(FIRST):
        d_copy(k, SHARED[0] <= k < SHARED[1]).start()

    to_core = y // 2
    w_slot = (y % 2) * 2 + c
    w_own = w_v.at[z, pl.ds(depth * y, depth), pl.ds(LANES * c, LANES)]

    def w_start(i):
        return remote(w_hbm, w_own, s_w.at[i], r_w.at[w_slot], 2 * z + to_core, y_peer(i))

    for i in range(1, SIDE):
        w_start(i).start()

    @pl.when(c == to_core)
    def _():
        pltpu.make_async_copy(w_hbm, w_own, r_w.at[w_slot]).start()

    @pl.when(c != to_core)
    def _():
        w_start(0).start()

    def x_block(row_y, column_y, g):
        to = (x + TO[g]) % SIDE
        return (
            x_hbm.at[pl.ds(quarter * row_y + own * to, own), :],
            xq.at[pl.ds(own * to, own), pl.ds(depth * column_y, depth)],
        )

    def x_copy(i, g):
        src, dst = x_block((y + i) % SIDE, y, g)
        return remote(src, dst, s_x.at[i, g], r_x.at[i, g], dp, y_peer(i))

    def x_arrival(i, g):
        _, dst = x_block(y, (y - i + SIDE) % SIDE, g)
        return remote(dst, dst, s_x.at[i, g], r_x.at[i, g], dp, me)

    xq_local = pltpu.make_async_copy(
        x_hbm.at[pl.ds(quarter * y, quarter), :], xq.at[:, pl.ds(depth * y, depth)], l_sem.at[2]
    )
    xq_local.start()

    half_u, quarter_u = up_rows // 2, up_rows // 4

    def u_part(block, par):
        return u_v.at[c, block, pl.ds(half_u * par, half_u), :]

    def u_copy(i):
        return remote(
            u_hbm.at[c, pl.ds(half_u * parity, half_u), :], u_part(y, parity),
            s_u.at[i], r_u.at[i], dp, y_peer(i),
        )

    def u_arrival(i):
        block = u_part((y - i + SIDE) % SIDE, parity)
        return remote(block, block, s_u.at[i], r_u.at[i], dp, me)

    def u_share(way, par):
        block = u_v.at[c, :, pl.ds(half_u * par + quarter_u * way, quarter_u), :]
        return remote(block, block, s_v.at[way], r_v.at[way], 2 * z_at(1 - 2 * way) + c, me)

    u_local = pltpu.make_async_copy(
        u_hbm.at[c, pl.ds(half_u * parity, half_u), :], u_part(y, parity), l_sem.at[3]
    )
    u_local.start()

    lane = lax.broadcasted_iota(jnp.int32, (LANES, LANES), 1)
    low_acc[...] = jnp.zeros_like(low_acc)

    def adapters(block):
        row = idx_ref[pl.ds(block, 1), :].astype(f32)
        return jnp.transpose(jnp.broadcast_to(row, (LANES, LANES))).astype(jnp.int32)

    @pl.loop(0, key_low.shape[0] // LANES)
    def _(b):
        a = adapters(b)
        key_low[pl.ds(pl.multiple_of(b * LANES, LANES), LANES), :] = jnp.where(
            (lane >> 5) == (a & 3), a >> 2, -1
        )

    @pl.loop(0, quarter // LANES)
    def _(b):
        a = adapters(y * (quarter // LANES) + b)
        owner = a >> 3
        mine = jnp.logical_and((owner & 3) == x, (lane >> 4) == (a & 7))
        key_up[pl.ds(pl.multiple_of(b * LANES, LANES), LANES), :] = jnp.where(mine, owner >> 2, -1)

    def piece(block, core, turn):
        return w_v.at[block, pl.ds(half_w * ((core + turn) % 2), half_w), :]

    def ring(j, turn, block):
        part = piece(block, c, turn)
        return remote(part, part, s_r.at[j, turn], r_r.at[j, turn], 2 * z_at(1 - 2 * c) + c, me)

    def share(t, turn, block, core):
        part = piece(block, core, turn)
        return remote(part, part, s_s.at[t, turn], r_s.at[t, turn], sib, me)

    def ring_start(turn):
        if turn == 0:
            for slot in range(4):
                block = w_v.at[
                    z, pl.ds(depth * (2 * c + slot // 2), depth), pl.ds(LANES * (slot % 2), LANES)
                ]
                remote(block, block, s_w.at[0], r_w.at[slot], dp, me).wait_recv()
            share(0, 0, z, c).start()
        else:
            share(0, 0, z, 1 - c).wait_recv()
        ring(1, turn, z).start()

    def ring_event(e):
        j, turn = e // 2 + 1, e % 2
        block = z_at(j * (2 * c - 1))
        ring(j, turn, block).wait_recv()

        @pl.when(e < EVENTS - 2)
        def _():
            ring(j + 1, turn, block).start()

        share(jnp.where(e < EVENTS - 1, 2 * j - 1 + c, EVENTS), turn, block, c).start()

    ring_start(0)
    for k in range(FIRST, WINDOW):
        d_copy(k, SHARED[0] <= k < SHARED[1]).start()

    def down_step(k, q):
        owner = jnp.where(k == 0, me, d_peer(jnp.maximum(k - 1, 0), -1))
        rows = pl.ds(pl.multiple_of(q * quarter, quarter), quarter)
        product = jnp.dot(x_v[rows, :], d_v[owner], preferred_element_type=f32)
        key = key_low[rows, :]
        low_acc[rows, :] = jnp.where(
            key == 2 * owner, product[:, :LANES],
            jnp.where(key == 2 * owner + 1, product[:, LANES:], low_acc[rows, :]),
        )

    def x_start(g):
        for i in range(1, SIDE):
            x_copy(i, g).start()

    x_local.wait()
    d_local.wait()

    @pl.loop(0, GROUP)
    def _(k):
        for e in range(len(RING_AT)):
            @pl.when(k == RING_AT[e])
            def _():
                ring_event(e)

        def arrive(shared):
            d_arrival(k, shared).wait_recv()
            d_forward(k, c, shared).start()
            if shared:
                for way in range(2):
                    d_share(k, way, parity).start()

        by_kind(k, 0, GROUP - 1, arrive)
        by_kind(k + WINDOW, WINDOW, GROUP - 1, lambda kind: d_copy(k + WINDOW, kind).start())

        @pl.when(k == HALF_AT)
        def _():
            ring_start(1)

        @pl.when(k == TOKENS_AT)
        def _():
            x_start(0)

        @pl.when(k == UP_AT)
        def _():
            for i in range(1, SIDE):
                u_copy(i).start()

        @pl.when(is_shared(k - Z_LAG))
        def _():
            for way in range(2):
                d_share(k - Z_LAG, way, 1 - parity).wait_recv()
            d_forward_other(k - Z_LAG, c).start()

        @pl.when(jnp.logical_not(is_shared(k - 1)))
        def _():
            @pl.when(k >= 1)
            def _():
                d_forward(k - 1, 1 - c, False).wait_recv()

            for q in range(SIDE):
                down_step(k, q)

    for k in range(*SHARED):
        d_forward(k, 1 - c, True).wait_recv()
        d_forward_other(k, 1 - c).wait_recv()
    first_event = len(RING_AT)

    lane_own = lax.broadcasted_iota(jnp.int32, (own, LANES), 1)

    def p_copy(i):
        return remote(p_send.at[(y + i) % SIDE], p_recv.at[i - 1], s_p.at[i], r_p.at[i], dp, y_peer(i))

    def q_copy(i):
        return remote(q_send, q_recv.at[i - 1], s_q.at[i], r_q.at[i], dp, x_peer(i))

    @pl.loop(1, SIDE + 1)
    def _(k):
        q = (y + k) % SIDE

        @pl.when(k == 1)
        def _():
            u_local.wait()
            for i in range(1, SIDE):
                u_arrival(i).wait_recv()
            for way in range(2):
                u_share(way, parity).start()

        for e in range(len(TAIL_AT)):
            @pl.when(k == TAIL_AT[e])
            def _():
                ring_event(first_event + e)

        for i in range(*SHARED):
            down_step(i + 1, q)

        packed = jnp.zeros((own, LANES), f32)
        for j in range(SIDE):
            v = low_acc[pl.ds(pl.multiple_of(q * quarter + j * own, own), own), :]
            v = v + pltpu.roll(v, 64, 1)
            v = v + pltpu.roll(v, 32, 1)
            packed = jnp.where((lane_own >> 5) == j, v, packed)
        p_send[q] = packed.astype(bf16)

        @pl.when(k == SIDE)
        def _():
            p_own[...] = packed

        @pl.when(k < SIDE)
        def _():
            remote(p_send.at[q], p_recv.at[k - 1], s_p.at[k], r_p.at[k], dp, y_peer(k)).start()

    for g in AFTER_DOWN:
        x_start(g)
    first_event += len(TAIL_AT)
    def u_forward(core):
        return remote(u_v.at[core], u_v.at[core], s_uf, r_uf, sib, me)

    def ring_events(first, count):
        for e in range(first, min(first + count, EVENTS)):
            ring_event(e)
        return min(first + count, EVENTS)

    first_event = ring_events(first_event, EXCHANGE_EVENTS[0])
    for i in range(1, SIDE):
        p_copy(i).wait_recv()
    p_sum = p_own[...]
    for i in range(SIDE - 1):
        p_sum = p_sum + p_recv[i].astype(f32)
    p_own[...] = p_sum
    q_send[...] = p_sum.astype(bf16)
    for i in range(1, SIDE):
        q_copy(i).start()
    for g in range(1 + len(AFTER_DOWN), SIDE):
        x_start(g)
    first_event = ring_events(first_event, EXCHANGE_EVENTS[1])
    for way in range(2):
        u_share(way, 1 - parity).wait_recv()
    u_forward(c).start()
    first_event = ring_events(first_event, EXCHANGE_EVENTS[2])
    for i in range(1, SIDE):
        q_copy(i).wait_recv()
    low = p_own[...]
    for i in range(SIDE - 1):
        low = low + q_recv[i].astype(f32)
    low = low.astype(bf16)
    low = (low.astype(f32) * ADAPTER_SCALE).astype(bf16)
    k_iota = lax.broadcasted_iota(jnp.int32, (LANES, LANES), 0)
    for j in range(SIDE):
        key = key_up[j * own:(j + 1) * own, :]
        for p in range(2):
            spread = (k_iota == 32 * j + 16 * p + (lane & 15)).astype(f32).astype(bf16)
            rows = jnp.dot(low, spread, preferred_element_type=f32)
            for g in range(SIDE):
                e_v[p, j * own:(j + 1) * own, g * LANES:(g + 1) * LANES] = jnp.where(
                    key == g, rows, 0.0
                ).astype(bf16)

    xq_local.wait()
    u_forward(1 - c).wait_recv()

    per_part = u_v.shape[3] // wide

    def block_at(t):
        return z_at(jnp.where(t % 2 == 1, -((t + 1) // 2), t // 2))

    def relay(t, n):
        to = jnp.where(t % 2 == 0, 1, SIDE - 1)
        return remote(relay_send.at[n], relay_recv.at[n], s_y.at[n], r_y.at[n], dp, x_peer(to))

    def o_copy(g, n):
        return remote(
            o_send.at[g - 1, n], o_recv.at[g - 1, n], s_o.at[g, n], r_o.at[g, n], dp, x_peer(TO[g])
        )

    seen = set()
    for events, g, first, end in SEGMENTS:
        if g not in seen:
            seen.add(g)
            for i in range(1, SIDE):
                x_arrival(i, g).wait_recv()
        first_event = ring_events(first_event, events)
        rows = pl.ds(pl.multiple_of(own * ((x + TO[g]) % SIDE), own), own)

        @pl.loop(first, end)
        def _(t):
            n = block_at(t)
            if g == 0:
                far = t == EVENTS

                @pl.when(jnp.logical_or(far, jnp.logical_and(t > 0, (t + 1) % 2 != c)))
                def _():
                    share(t, 0, n, 1 - c).wait_recv()

                    @pl.when(jnp.logical_not(far))
                    def _():
                        share(t, 1, n, 1 - c).wait_recv()
            p = n // per_part
            columns = pl.ds(pl.multiple_of((n % per_part) * wide, wide), wide)
            total = jnp.dot(xq[rows, :], w_v[n], preferred_element_type=f32) + jnp.dot(
                e_v[p, rows, :], u_v[p, :, :, columns].reshape(SIDE * up_rows, wide), preferred_element_type=f32
            )
            if g == 0:
                relay_send[n] = total.astype(bf16)
                relay(t, n).start()
            elif g == SIDE - 1:
                acc_v[n] = total
            else:
                mine = t % 2 == g - 1

                @pl.when(mine)
                def _():
                    relay(t, n).wait_recv()
                    o_send[g - 1, n] = (total + relay_recv[n].astype(f32)).astype(bf16)

                @pl.when(jnp.logical_not(mine))
                def _():
                    o_send[g - 1, n] = total.astype(bf16)

                o_copy(g, n).start()

    @pl.loop(0, chips)
    def _(t):
        n = block_at(t)
        for g in range(1, SIDE - 1):
            o_copy(g, n).wait_recv()
        total = acc_v[n] + (o_recv[0, n].astype(f32) + o_recv[1, n].astype(f32))
        out_ref[:, pl.ds(pl.multiple_of(wide * n, wide), wide)] = total.astype(bf16)

    for i in range(1, SIDE):
        w_start(i).wait_send()
        for g in range(SIDE):
            x_copy(i, g).wait_send()
        u_copy(i).wait_send()
        p_copy(i).wait_send()
        q_copy(i).wait_send()

    @pl.when(c != to_core)
    def _():
        w_start(0).wait_send()

    u_forward(c).wait_send()
    for way in range(2):
        u_share(way, parity).wait_send()

    @pl.loop(0, GROUP - 1)
    def _(k):
        def sent(shared):
            d_copy(k, shared).wait_send()
            d_forward(k, c, shared).wait_send()
            if shared:
                d_forward_other(k, c).wait_send()
                for way in range(2):
                    d_share(k, way, parity).wait_send()

        by_kind(k, 0, GROUP - 1, sent)

    for e in range(EVENTS):
        ring(e // 2 + 1, e % 2, z).wait_send()
        share(jnp.where(e < EVENTS - 1, 2 * (e // 2) + 1 + c, EVENTS), e % 2, z, c).wait_send()
    share(0, 0, z, c).wait_send()

    @pl.loop(0, chips)
    def _(t):
        relay(t, t).wait_send()
        for g in range(1, SIDE - 1):
            o_copy(g, t).wait_send()


def local(tokens, frozen_weight, adapter_down_weight, adapter_up_weight, token_adapter_index):
    rows, depth = tokens.shape
    core_columns = frozen_weight.shape[1]
    devices = lax.axis_size("dp")
    chips = devices // 2
    columns = devices * core_columns
    present, rank, span = adapter_up_weight.shape[1:]
    quarter, own = rows // SIDE, rows // GROUP
    owner_columns = adapter_down_weight.shape[1]
    f32, bf16 = jnp.float32, jnp.bfloat16
    idx = token_adapter_index.reshape(rows // LANES, LANES)
    up = adapter_up_weight.reshape(2, present * rank, span)
    anywhere = pl.BlockSpec(memory_space=pl.ANY)
    vmem = pl.BlockSpec(memory_space=pltpu.VMEM)
    dma = pltpu.SemaphoreType.DMA
    return pl.pallas_call(
        body,
        out_shape=jax.ShapeDtypeStruct((own, columns), bf16),
        in_specs=[vmem, anywhere, anywhere, anywhere, anywhere],
        out_specs=vmem,
        scratch_shapes=[
            pltpu.VMEM((rows, depth), bf16),
            pltpu.VMEM((quarter, SIDE * depth), bf16),
            pltpu.VMEM((chips, SIDE * depth, 2 * core_columns), bf16),
            pltpu.VMEM((GROUP, depth, owner_columns), bf16),
            pltpu.VMEM((2, SIDE, present * rank, span), bf16),
            pltpu.VMEM((rows, LANES), f32),
            pltpu.VMEM((rows, LANES), jnp.int32),
            pltpu.VMEM((quarter, LANES), jnp.int32),
            pltpu.VMEM((SIDE, own, LANES), bf16),
            pltpu.VMEM((SIDE - 1, own, LANES), bf16),
            pltpu.VMEM((own, LANES), bf16),
            pltpu.VMEM((SIDE - 1, own, LANES), bf16),
            pltpu.VMEM((own, LANES), f32),
            pltpu.VMEM((2, quarter, SIDE * present * rank), bf16),
            pltpu.VMEM((chips, own, 2 * core_columns), f32),
            pltpu.VMEM((2, chips, own, 2 * core_columns), bf16),
            pltpu.VMEM((2, chips, own, 2 * core_columns), bf16),
            pltpu.VMEM((chips, own, 2 * core_columns), bf16),
            pltpu.VMEM((chips, own, 2 * core_columns), bf16),
            dma((4,)),
            dma((GROUP,)), dma((GROUP,)), dma((GROUP, 2)), dma((GROUP, 2)), dma((GROUP, 2)), dma((GROUP, 2)),
            dma((4,)), dma((4,)), dma((SIDE, SIDE)), dma((SIDE, SIDE)), dma((SIDE,)), dma((SIDE,)), dma((2,)), dma((2,)),
            dma, dma,
            dma((chips, 2)), dma((chips, 2)), dma((chips, 2)), dma((chips, 2)),
            dma((SIDE,)), dma((SIDE,)), dma((SIDE,)), dma((SIDE,)),
            dma((SIDE, chips)), dma((SIDE, chips)), dma((chips,)), dma((chips,)),
        ],
        compiler_params=pltpu.CompilerParams(
            collective_id=0, has_side_effects=True, vmem_limit_bytes=60 << 20
        ),
        name="projections",
    )(idx, tokens, frozen_weight, adapter_down_weight, up)


def solution(mesh):
    placed = (P("dp", "mp"), P("mp", "dp"), P(None, "mp"), P(None, "mp", None, None), P("dp"))
    return jax.shard_map(
        local, mesh=mesh, in_specs=placed, out_specs=P(("dp", "mp"), None), check_vma=False
    )
```
